512 devices in a mesh: group: 16 (over z, core), sub: 32 (over x, y).
Axes of the slice: x: 4, y: 8, z: 8, core: 2. Of those that a mesh axis runs over, the one named last changes fastest.
Arguments:
- points: bfloat16 [32, 1048576], P(None, ('group', 'sub')), may hold values from -6 to 6
- charges: bfloat16 [16, 1048576], P(None, ('group', 'sub')), may hold values from -6 to 6
- leaf_order: int32 [1048576], P(('group', 'sub')), may hold values from 0 to 2047, as said below
- near_lists: int32 [4096, 7], P('group'), may hold values from 0 to 255, as said below
- far_lists: int32 [4096, 80], P(('group', 'sub')), may hold values from 0 to 255
- leaf_skeleton: int32 [4096, 128], P(('group', 'sub')), may hold values from 0 to 255, as said below
- leaf_interp: bfloat16 [4096, 128, 256], P(('group', 'sub')), may hold values from -0.375 to 0.375
- top_interp: bfloat16 [4096, 32768], P('group', 'sub'), may hold values from -0.1875 to 0.1875
- top_skeleton: int32 [16, 256], P('group'), may hold values from 0 to 2047, as said below
- top_owner: int32 [16], P('group'), may hold values from 0 to 31
- top_lists: int32 [16, 2], replicated, may hold values from 0 to 15, as said below
Outputs:
- potentials: float32 [16, 1048576], P(None, ('group', 'sub'))
The draws below stay inside these ranges and needn't reach their ends.
Inputs may be any that keep to these rules, and one draw needn't show every extreme that they name: `leaf_order`: each device's block of 2048 entries is a permutation of its positions. `near_lists`: entries are sub index times 8 plus leaf within the device. A leaf's 7 entries lie on different devices, none its own. Over the lists of all leaves of one device, at most 2 distinct leaves of any one other device appear. `leaf_skeleton`: each row holds 128 different positions. `top_skeleton`: each row holds 256 different positions. `top_lists`: each row holds 2 different groups, never its own.
All inputs are finite; a program needn't handle non-finite values.
Results may differ from the reference program's by a relative error of at most 0.005.
Values may be sent and summed in bfloat16 or wider, within the bound.
A program may use at most 64 MiB of HBM per device.

```python
import jax
import jax.numpy as jnp
from jax import lax

DIM = 32
RHS_COLUMNS = 16
LEAF = 256
LEAF_SKELETON_N = 128
NEAR = 7
FAR = 80
CAP = 2
TOPSKEL = 256
FAR_TOP = 2
LEAF_DEV = 8
N_POINTS = 1048576
LEAVES = 4096
TOP_ROWS = 4096
TOP_COLS = 32768
N_GROUP = 16
N_SUB = 32


def distinct_prefix(key, row_count, length, keep_count):
    scores = jax.random.randint(key, (row_count, length), 0, 1 << 16) * length + jnp.arange(length, dtype=jnp.int32)[None, :]
    ordering = jnp.argsort(scores, axis=1)
    return ordering[:, :keep_count].astype(jnp.int32)


def draw_leaf_order(key, part):
    pts_dev = LEAF_DEV * LEAF
    return distinct_prefix(key, N_GROUP * N_SUB, pts_dev, pts_dev).reshape(-1)


def draw_leaf_skeleton(key, part):
    return distinct_prefix(key, N_GROUP * N_SUB * LEAF_DEV, LEAF, LEAF_SKELETON_N)


def draw_top_skeleton(key, part):
    return distinct_prefix(key, N_GROUP, LEAF_DEV * LEAF, TOPSKEL)


def draw_top_lists(key, part):
    half_away = N_GROUP // 2
    others = max(N_GROUP - 2, 1)
    base_shift = jax.random.randint(key, (N_GROUP, 1), 0, others)
    groups = jnp.arange(N_GROUP, dtype=jnp.int32)[:, None]
    step_range = jnp.arange(FAR_TOP, dtype=jnp.int32)[None, :]
    offset = 1 + (base_shift + step_range - 1) % others
    offset = jnp.where(offset >= half_away, offset + 1, offset)
    offset = jnp.where(step_range == 0, half_away, offset)
    return ((groups + offset) % N_GROUP).astype(jnp.int32)


def draw_near_lists(key, part):
    key_base = jax.random.fold_in(key, 11)
    key_pick = jax.random.fold_in(key, 12)
    key_leaf = jax.random.fold_in(key, 13)
    grid_shape = (N_GROUP, N_SUB, LEAF_DEV)
    half_step = N_SUB // 2 - 1
    leaf_pos = jnp.arange(LEAF_DEV, dtype=jnp.int32)[None, None, :]
    base_shift = jax.random.randint(key_base, grid_shape, 0, N_SUB - 1)
    base_shift = jnp.where(leaf_pos < CAP, half_step, base_shift)
    pick_slot = jax.random.randint(key_pick, grid_shape + (NEAR,), 0, CAP)
    column = jnp.arange(NEAR, dtype=jnp.int32)
    forced = (leaf_pos[..., None] < CAP) & (column == 0)
    pick_slot = jnp.where(forced, jnp.broadcast_to(leaf_pos[..., None], pick_slot.shape), pick_slot)
    receiver = jnp.arange(N_SUB, dtype=jnp.int32)[None, :, None, None]
    sender = (receiver + 1 + (base_shift[..., None] + column * half_step) % (N_SUB - 1)) % N_SUB
    chosen = distinct_prefix(key_leaf, N_GROUP * N_SUB * N_SUB, LEAF_DEV, CAP).reshape(N_GROUP, N_SUB, N_SUB, CAP)
    group_pos = jnp.arange(N_GROUP, dtype=jnp.int32)[:, None, None, None]
    receiver_full = jnp.broadcast_to(receiver, sender.shape)
    leaf_of = chosen[group_pos, receiver_full, sender, pick_slot]
    return (sender * LEAF_DEV + leaf_of).reshape(N_GROUP * N_SUB * LEAF_DEV, NEAR).astype(jnp.int32)


def touch_ends(entries, key, smallest, high):
    index_at = [jax.random.randint(jax.random.fold_in(key, axis), (), 0, length) for axis, length in enumerate(entries.shape)]
    widest = entries.shape.index(max(entries.shape))
    neighbour = index_at[:widest] + [(index_at[widest] + 1) % entries.shape[widest]] + index_at[widest + 1:]
    return entries.at[tuple(index_at)].set(smallest).at[tuple(neighbour)].set(high)


def block_scale(own_key, dims, shards, least, high):
    loudness, own = 1.0, jax.random.fold_in(own_key, 6)
    for dim, blocks in shards:
        steps = jnp.exp(jax.random.uniform(jax.random.fold_in(own, dim), (blocks,), jnp.float32, least / len(shards), high / len(shards)))
        loudness = loudness * jnp.repeat(steps, dims[dim] // blocks).reshape([-1 if axis == dim else 1 for axis in range(len(dims))])
    return loudness


def scatter_about(key, extent, spread, most, shards=(), kind=jnp.bfloat16):
    drawn = spread * jax.random.normal(key, extent, jnp.float32)
    if shards:
        drawn = drawn * block_scale(key, extent, shards, -0.22, 0.18)
    return jnp.clip(drawn, -most, most).astype(kind)


def setup_inputs(seed: int = 0) -> dict:
    keys = jax.random.split(jax.random.key(seed), 12)
    points = scatter_about(keys[0], (DIM, N_POINTS), 1.0, 6.0, ((1, 512),))
    charges = scatter_about(keys[1], (RHS_COLUMNS, N_POINTS), 1.0, 6.0, ((1, 512),))
    leaf_order = draw_leaf_order(jax.random.fold_in(keys[11], 71), 0)
    near_lists = draw_near_lists(jax.random.fold_in(keys[11], 71), 0)
    far_lists = touch_ends(jax.random.randint(keys[4], (LEAVES, FAR), 0, N_SUB * LEAF_DEV), jax.random.fold_in(keys[4], 1), 0, (N_SUB * LEAF_DEV) - 1).astype(jnp.int32)
    leaf_skeleton = draw_leaf_skeleton(jax.random.fold_in(keys[11], 71), 0)
    leaf_interp = scatter_about(keys[6], (LEAVES, LEAF_SKELETON_N, LEAF), LEAF ** -0.5, 0.375, ((0, 512),))
    top_interp = scatter_about(keys[7], (TOP_ROWS, TOP_COLS), (LEAF_DEV * LEAF_SKELETON_N) ** -0.5, 0.1875, ((0, 16), (1, 32)))
    top_skeleton = draw_top_skeleton(jax.random.fold_in(keys[11], 71), 0)
    top_owner = touch_ends(jax.random.randint(keys[9], (N_GROUP,), 0, N_SUB), jax.random.fold_in(keys[9], 1), 0, N_SUB - 1).astype(jnp.int32)
    top_lists = draw_top_lists(jax.random.fold_in(keys[11], 71), 0)
    return {"points": points, "charges": charges, "leaf_order": leaf_order, "near_lists": near_lists, "far_lists": far_lists, "leaf_skeleton": leaf_skeleton, "leaf_interp": leaf_interp, "top_interp": top_interp, "top_skeleton": top_skeleton, "top_owner": top_owner, "top_lists": top_lists}


decay_rate = 3.0 ** 0.5 / 3.0
ridge_shift = 0.5
highest_level = lax.Precision.HIGHEST

def kernel_block(inner_products, norms_left, norms_right):
    distance_sq = jnp.maximum(norms_left[..., :, None] + norms_right[..., None, :] - 2.0 * inner_products, 0.0)
    scaled = jnp.sqrt(distance_sq) * decay_rate
    values = ((1.0 + scaled) * jnp.exp(-scaled)).astype(jnp.bfloat16)
    return lax.optimization_barrier(values).astype(jnp.float32)

def rounded_size(values):
    return lax.optimization_barrier(values.astype(jnp.bfloat16)).astype(jnp.float32)

def square_norms(values):
    return lax.optimization_barrier(jnp.sum(values * values, axis=-2))

def reference(points, charges, leaf_order, near_lists, far_lists, leaf_skeleton, leaf_interp, top_interp, top_skeleton, top_owner, top_lists):
    pts_dev = LEAF_DEV * LEAF
    n_points = points.shape[1]
    devices = N_GROUP * N_SUB
    group_leaves = N_SUB * LEAF_DEV
    leaf_nodes = devices * LEAF_DEV
    offsets = jnp.arange(n_points, dtype=jnp.int32) // pts_dev * pts_dev
    source = (offsets + leaf_order).astype(jnp.int32)
    tree_points = points.astype(jnp.float32)[:, source]
    tree_charges = charges.astype(jnp.float32)[:, source]
    leaf_coords = tree_points.reshape(DIM, leaf_nodes, LEAF).transpose(1, 0, 2)
    leaf_charges = tree_charges.reshape(RHS_COLUMNS, leaf_nodes, LEAF).transpose(1, 0, 2)
    leaf_ids = jnp.arange(leaf_nodes, dtype=jnp.int32)
    group_base = leaf_ids // group_leaves * group_leaves
    near_all = jnp.concatenate([leaf_ids[:, None], group_base[:, None] + near_lists], axis=1).astype(jnp.int32)
    far_all = (group_base[:, None] + far_lists).astype(jnp.int32)

    def near_block(block_index):
        first_leaf = (block_index * LEAF_DEV).astype(jnp.int32)
        own_coords = lax.dynamic_slice_in_dim(leaf_coords, first_leaf, LEAF_DEV, 0)
        indices = lax.dynamic_slice_in_dim(near_all, first_leaf, LEAF_DEV, 0)
        other_coords = leaf_coords[indices]
        other_charges = leaf_charges[indices]
        inner_products = jnp.einsum('lda,ljdb->ljab', own_coords, other_coords, precision=highest_level)
        blocks = kernel_block(inner_products, square_norms(own_coords)[:, None, :], square_norms(other_coords))
        return jnp.einsum('ljab,ljrb->lra', blocks, other_charges, precision=highest_level)
    near = lax.map(near_block, jnp.arange(devices, dtype=jnp.int32)).reshape(leaf_nodes, RHS_COLUMNS, LEAF)
    skel_charge = rounded_size(jnp.einsum('lsb,lrb->lrs', leaf_interp.astype(jnp.float32), leaf_charges, precision=highest_level))
    picker = jnp.broadcast_to(leaf_skeleton[:, None, :], (leaf_nodes, DIM, LEAF_SKELETON_N)).astype(jnp.int32)
    skel_points = jnp.take_along_axis(leaf_coords, picker, axis=2)

    def far_block(block_index):
        first_leaf = (block_index * LEAF_DEV).astype(jnp.int32)
        own_coords = lax.dynamic_slice_in_dim(skel_points, first_leaf, LEAF_DEV, 0)
        indices = lax.dynamic_slice_in_dim(far_all, first_leaf, LEAF_DEV, 0)
        other_coords = skel_points[indices]
        other_charges = skel_charge[indices]
        inner_products = jnp.einsum('lda,lfdb->lfab', own_coords, other_coords, precision=highest_level)
        blocks = kernel_block(inner_products, square_norms(own_coords)[:, None, :], square_norms(other_coords))
        return jnp.einsum('lfab,lfrb->lra', blocks, other_charges, precision=highest_level)
    far_field = lax.map(far_block, jnp.arange(devices, dtype=jnp.int32)).reshape(leaf_nodes, RHS_COLUMNS, LEAF_SKELETON_N)
    upper_weights = top_interp.astype(jnp.float32).reshape(N_GROUP, TOPSKEL, group_leaves, LEAF_SKELETON_N)
    clustered_charge = skel_charge.reshape(N_GROUP, group_leaves, RHS_COLUMNS, LEAF_SKELETON_N)
    cluster_charge = rounded_size(jnp.einsum('vlbx,vbyx->vyl', upper_weights, clustered_charge, precision=highest_level))
    owner_device = jnp.arange(N_GROUP, dtype=jnp.int32) * N_SUB + top_owner
    columns = (owner_device[:, None] * pts_dev + top_skeleton).astype(jnp.int32)
    group_points = tree_points[:, columns].transpose(1, 0, 2)
    other_points = group_points[top_lists]
    other_charge = cluster_charge[top_lists]
    inner_products = jnp.einsum('gda,gfdb->gfab', group_points, other_points, precision=highest_level)
    blocks = kernel_block(inner_products, square_norms(group_points)[:, None, :], square_norms(other_points))
    cluster_potential = rounded_size(jnp.einsum('gfab,gfrb->gra', blocks, other_charge, precision=highest_level))
    downward_pass = jnp.einsum('yfhv,yef->yhev', upper_weights, cluster_potential, precision=highest_level).reshape(leaf_nodes, RHS_COLUMNS, LEAF_SKELETON_N)
    skel_potential = rounded_size(far_field + downward_pass)
    tree_out = jnp.einsum('lsb,lrs->lrb', leaf_interp.astype(jnp.float32), skel_potential, precision=highest_level) + near + ridge_shift * leaf_charges
    tree_flat = tree_out.transpose(1, 0, 2).reshape(RHS_COLUMNS, n_points)
    return jnp.zeros((RHS_COLUMNS, n_points), jnp.float32).at[:, source].set(tree_flat)
```

```python
import functools

import jax
import jax.numpy as jnp
from jax import lax
from jax.experimental import pallas as pl
from jax.experimental.pallas import tpu as pltpu
from jax.sharding import PartitionSpec as P

MESH = pl.DeviceIdType.MESH
DECAY = 3.0**0.5 / 3.0
LOG2E = 1.4426950408889634
TINY = 1e-30
SHIFT = 0.5
DIMS, RHS, LEAF, SKEL, LEAVES, PTS = 32, 16, 256, 128, 8, 2048
NEAR, FAR, TOP = 7, 80, 256
NX, NY, GROUPS = 4, 8, 16
SUBS = NX * NY
SPLIT = 4
VMEM_LIMIT = 56 << 20


def nn(a, b):
    return lax.dot_general(a, b, (((1,), (0,)), ((), ())), preferred_element_type=jnp.float32)


def nt(a, b):
    return lax.dot_general(a, b, (((1,), (1,)), ((), ())), preferred_element_type=jnp.float32)


def bf(a):
    return a.astype(jnp.bfloat16)


def iota(shape, axis):
    return lax.broadcasted_iota(jnp.int32, shape, axis)


def hot(mask):
    return bf(jnp.where(mask, 1.0, 0.0))


def kernel_values(distance_sq):
    held = jnp.maximum(distance_sq, TINY)
    root = held * lax.rsqrt(held)
    return bf((1.0 + DECAY * root) * jnp.exp2((-DECAY * LOG2E) * root))


def norm_rows(points, first):
    wide = points.astype(jnp.float32)
    norm = jnp.sum(wide * wide, axis=0, keepdims=True)
    high = bf(norm).astype(jnp.float32)
    rest = norm - high
    mid = bf(rest).astype(jnp.float32)
    low = rest - mid
    row = iota((16, points.shape[1]), 0)
    parts = jnp.where(row == first, high, jnp.where(row == first + 1, mid, low))
    ours = (row >= first) & (row < first + 3)
    return bf(jnp.where(ours, parts, jnp.where(row < 6, 1.0, 0.0)))


def target_rows(points, eye):
    stacked = jnp.concatenate([bf(-2.0 * points.astype(jnp.float32)), norm_rows(points, 0)], axis=0)
    return bf(nt(eye, stacked))


def prepare(points, charges, order, skeleton, interp, top_interp, top_skeleton,
            far_pay, near_pay, far_targets, near_targets, tree_charges, message):
    both = jnp.concatenate([points[...], charges[...]], axis=0)
    eye = hot(iota((LEAF, LEAF), 0) == iota((LEAF, LEAF), 1))
    below = hot(iota((LEAF, LEAF), 1) < iota((LEAF, LEAF), 0))
    ones = jnp.ones((SKEL, SKEL), jnp.bfloat16)
    tree, skel_charges = [], []
    for leaf in range(LEAVES):
        row = order[:, leaf * LEAF:(leaf + 1) * LEAF]
        mine = bf(nn(both, hot(iota((PTS, LEAF), 0) == row)))
        mine_points, mine_charges = mine[:DIMS], mine[DIMS:]
        tree.append(mine_points)
        tree_charges[leaf] = mine_charges
        chosen = iota((LEAF, SKEL), 0) == skeleton[leaf:leaf + 1, :]
        taken = nn(hot(chosen), ones)
        rank = nn(below, bf(1.0 - taken))
        others = (rank == iota((LEAF, SKEL), 1).astype(jnp.float32)) & (taken == 0.0)
        moved = bf(nn(mine, jnp.concatenate([hot(chosen), hot(others)], axis=1)))
        skel_charge = bf(nt(mine_charges, interp[leaf]))
        skel_charges.append(skel_charge)
        skel_points = moved[:DIMS, :SKEL]
        far_pay[leaf, :DIMS] = skel_points
        far_pay[leaf, DIMS:] = skel_charge
        near_pay[leaf, :DIMS] = moved[:DIMS, SKEL:]
        near_pay[leaf, DIMS:DIMS + RHS] = moved[DIMS:, :SKEL]
        near_pay[leaf, DIMS + RHS:] = moved[DIMS:, SKEL:]
        near_targets[leaf] = target_rows(mine_points, eye)
        far_targets[leaf] = target_rows(skel_points, eye[:SKEL, :SKEL])
    all_charges = jnp.concatenate(skel_charges, axis=1)
    padded = jnp.concatenate([all_charges, jnp.zeros((128 - RHS, all_charges.shape[1]), jnp.bfloat16)], axis=0)
    partial = nt(top_interp[...], padded)
    all_points = jnp.concatenate(tree, axis=1)
    candidate = bf(nn(all_points, hot(iota((PTS, TOP), 0) == top_skeleton[...])))
    zeros = functools.partial(jnp.zeros, dtype=jnp.bfloat16)
    placed = jnp.concatenate([zeros((RHS, TOP)), candidate, zeros((128 - RHS - DIMS, TOP))], axis=0)
    message[...] = (partial + nt(eye, placed)).reshape(SUBS, 8, 128)


class Chain:
    def __init__(self, buf, sems, base, axis, wide, first, last):
        self.buf, self.sems, self.base = buf, sems, base
        self.axis, self.wide, self.first, self.last = axis, wide, first, last
        self.n = NY if axis == 1 else NX
        self.steps = self.n // 2
        self.count = 2 * self.steps

    def copy(self, way, step, incoming):
        x, y = lax.axis_index("sub") // NY, lax.rem(lax.axis_index("sub"), NY)
        me = y if self.axis == 1 else x
        sign = 1 if way == 0 else -1
        back = step if incoming else step - 1
        origin = lax.rem(me - sign * back + self.n, self.n)
        to = lax.rem(me + sign + self.n, self.n)
        first, last = self.first, self.last
        if step == self.steps:
            middle = (first + last + 1) // 2
            first, last = (first, middle) if way == 0 else (middle, last)
        leaves = pl.ds(first, last - first)
        if self.axis == 1:
            ref = self.buf.at[:, origin, leaves] if self.wide else self.buf.at[x, origin, leaves]
            target = x * NY + to
        else:
            ref = self.buf.at[origin, :, leaves] if self.wide else self.buf.at[origin, y, leaves]
            target = to * NY + y
        at = self.base + way * self.steps + step - 1
        send, recv = self.sems
        return pltpu.make_async_remote_copy(
            src_ref=ref, dst_ref=ref, send_sem=send.at[at], recv_sem=recv.at[at],
            device_id=(lax.axis_index("group"), target), device_id_type=MESH)

    def start(self, step):
        for way in range(2):
            self.copy(way, step, False).start()

    def arrive(self, step):
        for way in range(2):
            self.copy(way, step, True).wait_recv()

    def next(self, step):
        for way in range(2):
            self.copy(way, step, True).wait_recv()
            self.copy(way, step + 1, False).start()

    def sent(self):
        for step in range(1, self.steps + 1):
            for way in range(2):
                self.copy(way, step, False).wait_send()


PER_PAY = 2 * (NX + NY)


def chains(buf, sems, base):
    out = []
    for axis, wide, first, last in ((0, False, 0, SPLIT), (1, False, SPLIT, LEAVES), (1, True, 0, SPLIT),
                                    (0, True, SPLIT, LEAVES)):
        out.append(Chain(buf, sems, base, axis, wide, first, last))
        base += out[-1].count
    return out


def main(far_lists, near_lists, top_owner, top_lists,
         far_pay, near_pay, far_targets, near_targets, tree_charges, message, interp, top_interp, order,
         out,
         far_buf, near_buf, rows_buf, far_sum, near_sum, back_buf, shares, mine_top, pieces, packed, whole,
         send, recv, top_send, top_recv):
    sub, group = lax.axis_index("sub"), lax.axis_index("group")
    x, y = sub // NY, lax.rem(sub, NY)

    barrier = pltpu.get_barrier_semaphore()

    def greet_sub(j, carry):
        pl.semaphore_signal(barrier, inc=1, device_id=(group, lax.rem(sub + j, SUBS)), device_id_type=MESH)
        return carry

    def greet_group(j, carry):
        pl.semaphore_signal(barrier, inc=1, device_id=(lax.rem(group + j, GROUPS), sub), device_id_type=MESH)
        return carry

    lax.fori_loop(1, SUBS, greet_sub, 0)
    lax.fori_loop(1, GROUPS, greet_group, 0)
    far_buf[x, y] = far_pay[...]
    near_buf[x, y] = near_pay[...]
    shares[sub] = message[sub]
    pl.semaphore_wait(barrier, SUBS + GROUPS - 2)

    fx, fy, fyy, fxx = chains(far_buf, (send, recv), 0)
    nx, ny, nyy, nxx = chains(near_buf, (send, recv), PER_PAY)

    def to_sub(level, src, dst):
        def go(j, carry):
            peer = lax.rem(sub + j, SUBS)
            pltpu.make_async_remote_copy(
                src_ref=src(peer), dst_ref=dst.at[sub], send_sem=top_send.at[level], recv_sem=top_recv.at[level],
                device_id=(group, peer), device_id_type=MESH).start()
            return carry
        lax.fori_loop(1, SUBS, go, 0)

    def all_of(level, dst, count):
        ref = dst.at[pl.ds(0, count)]
        return pltpu.make_async_remote_copy(
            src_ref=ref, dst_ref=ref, send_sem=top_send.at[level], recv_sem=top_recv.at[level],
            device_id=(group, lax.rem(sub + 1, SUBS)), device_id_type=MESH)

    lane = iota((8, 128), 1)

    def top_first():
        to_sub(0, lambda peer: message.at[peer], shares)

    def top_second():
        all_of(0, shares, SUBS - 1).wait_recv()
        total = jnp.sum(shares[...], axis=0)
        chosen = shares[top_owner[0]]
        chunk = jnp.where(lane < RHS, bf(total).astype(jnp.float32), chosen)
        mine_top[...] = chunk
        pieces[group] = chunk

        def go(j, carry):
            pltpu.make_async_remote_copy(
                src_ref=mine_top, dst_ref=pieces.at[group], send_sem=top_send.at[1], recv_sem=top_recv.at[1],
                device_id=(lax.rem(group + j, GROUPS), sub), device_id_type=MESH).start()
            return carry
        lax.fori_loop(1, GROUPS, go, 0)

    def top_third():
        all_of(1, pieces, GROUPS - 1).wait_recv()
        one = pieces[top_lists[group, 0]]
        two = pieces[top_lists[group, 1]]
        row = jnp.where(lane < 48, one, jnp.where(lane < 96, pltpu.roll(two, 48, 1), pltpu.roll(mine_top[...], 80, 1)))
        packed[...] = row
        whole[sub] = row
        to_sub(2, lambda peer: packed, whole)

    fx.start(1)
    fy.start(1)
    top_first()
    fx.next(1)
    nx.start(1)
    fy.next(1)
    fx.arrive(2)
    fy.next(2)
    fyy.start(1)
    fy.next(3)
    nx.next(1)
    fy.arrive(4)
    fxx.start(1)
    top_second()
    ny.start(1)
    fyy.next(1)
    fxx.next(1)
    ny.next(1)
    fyy.next(2)
    top_third()
    ny.next(2)
    fyy.next(3)
    ny.next(3)
    nx.arrive(2)
    nyy.start(1)
    fxx.arrive(2)
    fyy.arrive(4)
    ny.arrive(4)
    nxx.start(1)

    def fill_rows(dev, carry):
        for leaf in range(LEAVES):
            rows_buf[dev // NY, lax.rem(dev, NY), leaf] = norm_rows(
                far_buf[dev // NY, lax.rem(dev, NY), leaf, :DIMS], 3)
        return carry

    lax.fori_loop(0, SUBS, fill_rows, 0)

    def place(index):
        return index // (NY * LEAVES), lax.rem(index // LEAVES, NY), lax.rem(index, LEAVES)

    def far_leaf(leaf, carry):
        @pl.when(leaf == 2)
        def _():
            nyy.next(1)

        @pl.when(leaf == 4)
        def _():
            nyy.next(2)
            nxx.next(1)

        @pl.when(leaf == 6)
        def _():
            nyy.next(3)

        sources, charges = [], []
        for entry in range(FAR):
            a, b, c = place(far_lists[leaf, entry])
            got = far_buf[a, b, c]
            sources.append(jnp.concatenate([got[:DIMS], rows_buf[a, b, c]], axis=0))
            charges.append(got[DIMS:])
        values = kernel_values(nn(far_targets[leaf], jnp.concatenate(sources, axis=1)))
        far_sum[leaf] = nt(jnp.concatenate(charges, axis=1), values)
        return carry

    lax.fori_loop(0, LEAVES, far_leaf, 0)
    nyy.arrive(4)
    nxx.arrive(2)

    def near_leaf(leaf, carry):
        sources, charges = [], []
        for entry in range(NEAR + 1):
            index = sub * LEAVES + leaf if entry == 0 else near_lists[sub * LEAVES + leaf, entry - 1]
            a, b, c = place(index)
            got = near_buf[a, b, c]
            sources.append(jnp.concatenate([far_buf[a, b, c, :DIMS], rows_buf[a, b, c]], axis=0))
            sources.append(jnp.concatenate([got[:DIMS], norm_rows(got[:DIMS], 3)], axis=0))
            charges.append(got[DIMS:DIMS + RHS])
            charges.append(got[DIMS + RHS:])
        values = kernel_values(nn(near_targets[leaf], jnp.concatenate(sources, axis=1)))
        near_sum[leaf] = nt(jnp.concatenate(charges, axis=1), values)
        return carry

    lax.fori_loop(0, LEAVES, near_leaf, 0)

    all_of(2, whole, SUBS - 1).wait_recv()
    table = whole[...].reshape(TOP, 128)
    narrow = bf(table)
    lanes = iota((TOP, 128), 1)
    squares = table * table
    square_high = bf(squares)
    square_low = bf(squares - square_high.astype(jnp.float32))
    own_norm = jnp.sum(jnp.where(lanes >= 96, squares, 0.0), axis=1, keepdims=True)
    potential = jnp.zeros((RHS, TOP), jnp.float32)
    for which in range(2):
        start = 48 * which
        points_at = (lanes >= start + RHS) & (lanes < start + 48)
        aligned = pltpu.roll(table, (start + RHS - 96) % 128, 1)
        left = bf(jnp.where(points_at, -2.0 * aligned, 0.0))
        flags = hot((iota((8, 128), 1) >= start + RHS) & (iota((8, 128), 1) < start + 48))
        other_norm = nt(flags, square_high) + nt(flags, square_low)
        values = kernel_values(nt(left, narrow) + own_norm + other_norm[:1])
        pick = hot(iota((RHS, 128), 1) == iota((RHS, 128), 0) + start)
        potential = potential + nt(bf(nt(pick, narrow)), values)
    down = nn(bf(potential), top_interp[...])

    for leaf in range(LEAVES):
        skel_potential = bf(far_sum[leaf] + down[:, leaf * SKEL:(leaf + 1) * SKEL])
        total = nn(skel_potential, interp[leaf]) + near_sum[leaf] + SHIFT * tree_charges[leaf].astype(jnp.float32)
        high = bf(total)
        rest = total - high.astype(jnp.float32)
        mid = bf(rest)
        low = bf(rest - mid.astype(jnp.float32))
        back_buf[:, leaf * LEAF:(leaf + 1) * LEAF] = jnp.concatenate([high, mid, low], axis=0)

    for tile in range(PTS // LEAF):
        take = hot(iota((LEAF, PTS), 0) + tile * LEAF == order[...])
        got = nt(back_buf[...], take)
        out[:, tile * LEAF:(tile + 1) * LEAF] = got[:RHS] + got[RHS:2 * RHS] + got[2 * RHS:]

    for chain in (fx, fy, fyy, fxx, nx, ny, nyy, nxx):
        chain.sent()
    all_of(0, shares, SUBS - 1).wait_send()
    all_of(1, pieces, GROUPS - 1).wait_send()
    all_of(2, whole, SUBS - 1).wait_send()


def body(points, charges, leaf_order, near_lists, far_lists, leaf_skeleton, leaf_interp, top_interp, top_skeleton,
         top_owner, top_lists):
    order = leaf_order.reshape(1, PTS)
    vmem, smem = pl.BlockSpec(memory_space=pltpu.VMEM), pl.BlockSpec(memory_space=pltpu.SMEM)
    shape = jax.ShapeDtypeStruct
    prepared = pl.pallas_call(
        prepare,
        out_shape=(
            shape((LEAVES, DIMS + RHS, SKEL), jnp.bfloat16),
            shape((LEAVES, DIMS + 2 * RHS, SKEL), jnp.bfloat16),
            shape((LEAVES, SKEL, DIMS + 16), jnp.bfloat16),
            shape((LEAVES, LEAF, DIMS + 16), jnp.bfloat16),
            shape((LEAVES, RHS, LEAF), jnp.bfloat16),
            shape((SUBS, 8, 128), jnp.float32),
        ),
        in_specs=[vmem] * 7,
        out_specs=(vmem,) * 6,
        compiler_params=pltpu.CompilerParams(vmem_limit_bytes=VMEM_LIMIT),
        name="prepare",
    )(points, charges, order, leaf_skeleton, leaf_interp, top_interp, top_skeleton)
    return pl.pallas_call(
        main,
        out_shape=shape((RHS, PTS), jnp.float32),
        in_specs=[smem] * 4 + [vmem] * 9,
        out_specs=vmem,
        scratch_shapes=[
            pltpu.VMEM((NX, NY, LEAVES, DIMS + RHS, SKEL), jnp.bfloat16),
            pltpu.VMEM((NX, NY, LEAVES, DIMS + 2 * RHS, SKEL), jnp.bfloat16),
            pltpu.VMEM((NX, NY, LEAVES, 16, SKEL), jnp.bfloat16),
            pltpu.VMEM((LEAVES, RHS, SKEL), jnp.float32),
            pltpu.VMEM((LEAVES, RHS, LEAF), jnp.float32),
            pltpu.VMEM((3 * RHS, PTS), jnp.bfloat16),
            pltpu.VMEM((SUBS, 8, 128), jnp.float32),
            pltpu.VMEM((8, 128), jnp.float32),
            pltpu.VMEM((GROUPS, 8, 128), jnp.float32),
            pltpu.VMEM((8, 128), jnp.float32),
            pltpu.VMEM((SUBS, 8, 128), jnp.float32),
            pltpu.SemaphoreType.DMA((2 * PER_PAY,)),
            pltpu.SemaphoreType.DMA((2 * PER_PAY,)),
            pltpu.SemaphoreType.DMA((3,)),
            pltpu.SemaphoreType.DMA((3,)),
        ],
        compiler_params=pltpu.CompilerParams(
            vmem_limit_bytes=VMEM_LIMIT, collective_id=0, has_side_effects=True),
        name="gather_and_sum",
    )(far_lists, near_lists, top_owner, top_lists, *prepared, leaf_interp, top_interp, order)


def solution(mesh):
    placed = (
        P(None, ("group", "sub")),
        P(None, ("group", "sub")),
        P(("group", "sub")),
        P("group", None),
        P(("group", "sub"), None),
        P(("group", "sub"), None),
        P(("group", "sub"), None, None),
        P("group", "sub"),
        P("group", None),
        P("group"),
        P(),
    )
    return jax.shard_map(
        body, mesh=mesh, in_specs=placed, out_specs=P(None, ("group", "sub")), check_vma=False
    )
```

```python
import functools

import jax
import jax.numpy as jnp
from jax import lax
from jax.experimental import pallas as pl
from jax.experimental.pallas import tpu as pltpu
from jax.sharding import PartitionSpec as P

MESH = pl.DeviceIdType.MESH
DECAY = 3.0**0.5 / 3.0
LOG2E = 1.4426950408889634
TINY = 1e-30
SHIFT = 0.5
DIMS, RHS, LEAF, SKEL, LEAVES, PTS = 32, 16, 256, 128, 8, 2048
NEAR, FAR, TOP, CAP = 7, 80, 256, 2
NX, NY, GROUPS = 4, 8, 16
SUBS = NX * NY
SPLIT = 2
VMEM_LIMIT = 56 << 20


def nn(a, b):
    return lax.dot_general(a, b, (((1,), (0,)), ((), ())), preferred_element_type=jnp.float32)


def nt(a, b):
    return lax.dot_general(a, b, (((1,), (1,)), ((), ())), preferred_element_type=jnp.float32)


def bf(a):
    return a.astype(jnp.bfloat16)


def iota(shape, axis):
    return lax.broadcasted_iota(jnp.int32, shape, axis)


def hot(mask):
    return bf(jnp.where(mask, 1.0, 0.0))


def kernel_values(distance_sq):
    held = jnp.maximum(distance_sq, TINY)
    root = held * lax.rsqrt(held)
    return bf((1.0 + DECAY * root) * jnp.exp2((-DECAY * LOG2E) * root))


def norm_rows(points, first):
    wide = points.astype(jnp.float32)
    norm = jnp.sum(wide * wide, axis=0, keepdims=True)
    high = bf(norm).astype(jnp.float32)
    rest = norm - high
    mid = bf(rest).astype(jnp.float32)
    low = rest - mid
    row = iota((16, points.shape[1]), 0)
    parts = jnp.where(row == first, high, jnp.where(row == first + 1, mid, low))
    ours = (row >= first) & (row < first + 3)
    return bf(jnp.where(ours, parts, jnp.where(row < 6, 1.0, 0.0)))


def target_rows(points, eye):
    stacked = jnp.concatenate([bf(-2.0 * points.astype(jnp.float32)), norm_rows(points, 0)], axis=0)
    return bf(nt(eye, stacked))


def near_tables(near, tables):
    sub = lax.axis_index("sub")
    entries = near[...]
    owner, leaf = entries // LEAVES, lax.rem(entries, LEAVES)
    ours = owner == sub
    least = jnp.min(jnp.where(ours, leaf, LEAVES), axis=0, keepdims=True)
    most = jnp.max(jnp.where(ours, leaf, -1), axis=0, keepdims=True)
    width = SUBS * LEAVES
    for shift in (1, 2, 4):
        least = jnp.minimum(least, pltpu.roll(least, width - shift, 1))
        most = jnp.maximum(most, pltpu.roll(most, width - shift, 1))
    tables[0:1, :] = jnp.where(least < LEAVES, least, 0)
    tables[1:2, :] = jnp.maximum(most, 0)
    mine = pltpu.roll(entries, lax.rem(width - sub * LEAVES, width), 1)[:, :128]
    mine = jnp.where(iota((NEAR, 128), 1) < LEAVES, mine, -1)
    sender = iota((SUBS, 128), 0)
    first = jnp.full((SUBS, 128), LEAVES, jnp.int32)
    rows = []
    for column in range(NEAR):
        row = mine[column:column + 1]
        rows.append((row >> 3 == sender, row & 7, row >> 3))
        first = jnp.minimum(first, jnp.where(rows[-1][0], rows[-1][1], LEAVES))
    first = jnp.min(first, axis=1, keepdims=True)
    for column, (match, leaf, owner) in enumerate(rows):
        lowest = jnp.sum(jnp.where(match, first, 0), axis=0, keepdims=True)
        slot = jnp.where(leaf == lowest, 0, 1)
        tables[2 + column:3 + column, 0:128] = jnp.where(owner >= 0, owner * CAP + slot, 0)


def prepare(points, charges, order, skeleton, interp, top_interp, top_skeleton, near,
            far_pay, near_pay, far_targets, near_targets, tree_charges, message, tables):
    near_tables(near, tables)
    both = jnp.concatenate([points[...], charges[...]], axis=0)
    eye = hot(iota((LEAF, LEAF), 0) == iota((LEAF, LEAF), 1))
    below = hot(iota((LEAF, LEAF), 1) < iota((LEAF, LEAF), 0))
    ones = jnp.ones((SKEL, SKEL), jnp.bfloat16)
    tree, skel_charges = [], []
    for leaf in range(LEAVES):
        row = order[:, leaf * LEAF:(leaf + 1) * LEAF]
        mine = bf(nn(both, hot(iota((PTS, LEAF), 0) == row)))
        mine_points, mine_charges = mine[:DIMS], mine[DIMS:]
        tree.append(mine_points)
        tree_charges[leaf] = mine_charges
        chosen = iota((LEAF, SKEL), 0) == skeleton[leaf:leaf + 1, :]
        taken = nn(hot(chosen), ones)
        rank = nn(below, bf(1.0 - taken))
        others = (rank == iota((LEAF, SKEL), 1).astype(jnp.float32)) & (taken == 0.0)
        moved = bf(nn(mine, jnp.concatenate([hot(chosen), hot(others)], axis=1)))
        skel_charge = bf(nt(mine_charges, interp[leaf]))
        skel_charges.append(skel_charge)
        skel_points = moved[:DIMS, :SKEL]
        far_pay[leaf, :DIMS] = skel_points
        far_pay[leaf, DIMS:] = skel_charge
        near_pay[leaf, :DIMS] = moved[:DIMS, SKEL:]
        near_pay[leaf, DIMS:DIMS + RHS] = moved[DIMS:, :SKEL]
        near_pay[leaf, DIMS + RHS:] = moved[DIMS:, SKEL:]
        near_targets[leaf] = target_rows(mine_points, eye)
        far_targets[leaf] = target_rows(skel_points, eye[:SKEL, :SKEL])
    all_charges = jnp.concatenate(skel_charges, axis=1)
    padded = jnp.concatenate([all_charges, jnp.zeros((128 - RHS, all_charges.shape[1]), jnp.bfloat16)], axis=0)
    partial = nt(top_interp[...], padded)
    all_points = jnp.concatenate(tree, axis=1)
    candidate = bf(nn(all_points, hot(iota((PTS, TOP), 0) == top_skeleton[...])))
    zeros = functools.partial(jnp.zeros, dtype=jnp.bfloat16)
    placed = jnp.concatenate([zeros((RHS, TOP)), candidate, zeros((128 - RHS - DIMS, TOP))], axis=0)
    message[...] = (partial + nt(eye, placed)).reshape(SUBS, 8, 128)


class Chain:
    def __init__(self, buf, sems, base, axis, wide, first, last, turn=0):
        self.buf, self.sems, self.base, self.turn = buf, sems, base, turn
        self.axis, self.wide, self.first, self.last = axis, wide, first, last
        self.n = NY if axis == 1 else NX
        self.steps = self.n // 2
        self.count = 2 * self.steps

    def copy(self, way, step, incoming):
        x, y = lax.axis_index("sub") // NY, lax.rem(lax.axis_index("sub"), NY)
        me = y if self.axis == 1 else x
        sign = 1 if way == 0 else -1
        back = step if incoming else step - 1
        origin = lax.rem(me - sign * back + self.n, self.n)
        to = lax.rem(me + sign + self.n, self.n)
        first, last = self.first, self.last
        if step == self.steps:
            middle = (first + last + 1) // 2
            first, last = (first, middle) if way == 0 else (middle, last)
        leaves = pl.ds(first, last - first)
        if self.axis == 1:
            ref = self.buf.at[:, origin, leaves] if self.wide else self.buf.at[x, origin, leaves]
            target = x * NY + to
        else:
            ref = self.buf.at[origin, lax.rem(y + self.turn, NY), leaves]
            target = to * NY + y
        at = self.base + way * self.steps + step - 1
        send, recv = self.sems
        return pltpu.make_async_remote_copy(
            src_ref=ref, dst_ref=ref, send_sem=send.at[at], recv_sem=recv.at[at],
            device_id=(lax.axis_index("group"), target), device_id_type=MESH)

    def start(self, step):
        for way in range(2):
            self.copy(way, step, False).start()

    def arrive(self, step):
        for way in range(2):
            self.copy(way, step, True).wait_recv()

    def next(self, step):
        for way in range(2):
            self.copy(way, step, True).wait_recv()
            self.copy(way, step + 1, False).start()

    def sent(self):
        for step in range(1, self.steps + 1):
            for way in range(2):
                self.copy(way, step, False).wait_send()


COPIES = 2 * NX // 2 + 2 * NY + NY * NX


def main(far_lists, near_lists, top_owner, top_lists, tables,
         far_pay, near_pay, far_targets, near_targets, tree_charges, message, interp, top_interp,
         out,
         far_buf, near_out, near_buf, rows_buf, far_sum, near_sum, shares, mine_top, pieces, packed, whole,
         send, recv, side_send, side_recv):
    sub, group = lax.axis_index("sub"), lax.axis_index("group")
    x, y = sub // NY, lax.rem(sub, NY)

    barrier = pltpu.get_barrier_semaphore()

    def greet_sub(j, carry):
        pl.semaphore_signal(barrier, inc=1, device_id=(group, lax.rem(sub + j, SUBS)), device_id_type=MESH)
        return carry

    def greet_group(j, carry):
        pl.semaphore_signal(barrier, inc=1, device_id=(lax.rem(group + j, GROUPS), sub), device_id_type=MESH)
        return carry

    lax.fori_loop(1, SUBS, greet_sub, 0)
    lax.fori_loop(1, GROUPS, greet_group, 0)
    far_buf[x, y] = far_pay[...]
    shares[sub] = message[sub]
    pl.semaphore_wait(barrier, SUBS + GROUPS - 2)

    sems = (send, recv)
    fx = Chain(far_buf, sems, 0, 0, False, 0, SPLIT)
    fy = Chain(far_buf, sems, fx.count, 1, False, SPLIT, LEAVES)
    fyy = Chain(far_buf, sems, fx.count + fy.count, 1, True, 0, SPLIT)
    base = fx.count + fy.count + fyy.count
    across = [Chain(far_buf, sems, base + turn * NX, 0, False, SPLIT, LEAVES, turn) for turn in range(NY)]

    def across_start(*turns):
        for turn in turns:
            across[turn].start(1)

    def across_next(*turns):
        for turn in turns:
            across[turn].next(1)

    def to_sub(level, src, dst):
        def go(j, carry):
            peer = lax.rem(sub + j, SUBS)
            pltpu.make_async_remote_copy(
                src_ref=src(peer), dst_ref=dst.at[sub], send_sem=side_send.at[level], recv_sem=side_recv.at[level],
                device_id=(group, peer), device_id_type=MESH).start()
            return carry
        lax.fori_loop(1, SUBS, go, 0)

    def all_of(level, dst, count):
        ref = dst.at[pl.ds(0, count)]
        return pltpu.make_async_remote_copy(
            src_ref=ref, dst_ref=ref, send_sem=side_send.at[level], recv_sem=side_recv.at[level],
            device_id=(group, lax.rem(sub + 1, SUBS)), device_id_type=MESH)

    lane = iota((8, 128), 1)

    def top_first():
        to_sub(0, lambda peer: message.at[peer], shares)

    def top_second():
        all_of(0, shares, SUBS - 1).wait_recv()
        total = jnp.sum(shares[...], axis=0)
        chosen = shares[top_owner[0]]
        chunk = jnp.where(lane < RHS, bf(total).astype(jnp.float32), chosen)
        mine_top[...] = chunk
        pieces[group] = chunk

        def go(j, carry):
            pltpu.make_async_remote_copy(
                src_ref=mine_top, dst_ref=pieces.at[group], send_sem=side_send.at[1], recv_sem=side_recv.at[1],
                device_id=(lax.rem(group + j, GROUPS), sub), device_id_type=MESH).start()
            return carry
        lax.fori_loop(1, GROUPS, go, 0)

    def top_third():
        all_of(1, pieces, GROUPS - 1).wait_recv()
        one = pieces[top_lists[0, group]]
        two = pieces[top_lists[1, group]]
        row = jnp.where(lane < 48, one, jnp.where(lane < 96, pltpu.roll(two, 48, 1), pltpu.roll(mine_top[...], 80, 1)))
        packed[...] = row
        whole[sub] = row
        to_sub(2, lambda peer: packed, whole)

    fx.start(1)
    fy.start(1)
    across_start(0)
    top_first()
    fx.next(1)

    def pick_near(peer, carry):
        for slot in range(CAP):
            near_out[peer, slot] = near_pay[tables[slot, peer * LEAVES]]
        return carry

    lax.fori_loop(0, SUBS, pick_near, 0)
    fy.next(1)
    across_start(1, NY - 1)
    across_next(0)
    fx.arrive(2)
    fy.next(2)
    fyy.start(1)
    across_start(2, NY - 2)
    across_next(1, NY - 1)
    fy.next(3)
    across_start(3, NY - 3)
    top_second()
    fy.arrive(4)
    across_start(4)
    fyy.next(1)
    across_next(2, NY - 2)
    fyy.next(2)
    across_next(3, NY - 3)
    top_third()
    fyy.next(3)
    across_next(4)
    to_sub(3, lambda peer: near_out.at[peer], near_buf)
    fyy.arrive(4)
    for turn in range(NY):
        across[turn].arrive(2)

    def fill_rows(dev, carry):
        for leaf in range(LEAVES):
            rows_buf[dev // NY, lax.rem(dev, NY), leaf] = norm_rows(
                far_buf[dev // NY, lax.rem(dev, NY), leaf, :DIMS], 3)
        return carry

    lax.fori_loop(0, SUBS, fill_rows, 0)

    def place(index):
        return index // (NY * LEAVES), lax.rem(index // LEAVES, NY), lax.rem(index, LEAVES)

    def far_leaf(leaf, carry):
        sources, charges = [], []
        for entry in range(FAR):
            a, b, c = place(far_lists[leaf, entry])
            got = far_buf[a, b, c]
            sources.append(jnp.concatenate([got[:DIMS], rows_buf[a, b, c]], axis=0))
            charges.append(got[DIMS:])
        values = kernel_values(nn(far_targets[leaf], jnp.concatenate(sources, axis=1)))
        far_sum[leaf] = nt(jnp.concatenate(charges, axis=1), values)
        return carry

    lax.fori_loop(0, LEAVES, far_leaf, 0)
    all_of(3, near_buf, SUBS - 1).wait_recv()

    def near_leaf(leaf, carry):
        sources, charges = [], []
        for entry in range(NEAR + 1):
            if entry == 0:
                a, b, c = x, y, leaf
                got = near_pay[leaf]
            else:
                a, b, c = place(near_lists[entry - 1, sub * LEAVES + leaf])
                at = tables[entry + 1, leaf]
                got = near_buf[at // CAP, lax.rem(at, CAP)]
            sources.append(jnp.concatenate([far_buf[a, b, c, :DIMS], rows_buf[a, b, c]], axis=0))
            sources.append(jnp.concatenate([got[:DIMS], norm_rows(got[:DIMS], 3)], axis=0))
            charges.append(got[DIMS:DIMS + RHS])
            charges.append(got[DIMS + RHS:])
        values = kernel_values(nn(near_targets[leaf], jnp.concatenate(sources, axis=1)))
        near_sum[leaf] = nt(jnp.concatenate(charges, axis=1), values)
        return carry

    lax.fori_loop(0, LEAVES, near_leaf, 0)

    all_of(2, whole, SUBS - 1).wait_recv()
    table = whole[...].reshape(TOP, 128)
    narrow = bf(table)
    lanes = iota((TOP, 128), 1)
    squares = table * table
    square_high = bf(squares)
    square_low = bf(squares - square_high.astype(jnp.float32))
    own_norm = jnp.sum(jnp.where(lanes >= 96, squares, 0.0), axis=1, keepdims=True)
    potential = jnp.zeros((RHS, TOP), jnp.float32)
    for which in range(2):
        start = 48 * which
        points_at = (lanes >= start + RHS) & (lanes < start + 48)
        aligned = pltpu.roll(table, (start + RHS - 96) % 128, 1)
        left = bf(jnp.where(points_at, -2.0 * aligned, 0.0))
        flags = hot((iota((8, 128), 1) >= start + RHS) & (iota((8, 128), 1) < start + 48))
        other_norm = nt(flags, square_high) + nt(flags, square_low)
        values = kernel_values(nt(left, narrow) + own_norm + other_norm[:1])
        pick = hot(iota((RHS, 128), 1) == iota((RHS, 128), 0) + start)
        potential = potential + nt(bf(nt(pick, narrow)), values)
    down = nn(bf(potential), top_interp[...])

    for leaf in range(LEAVES):
        skel_potential = bf(far_sum[leaf] + down[:, leaf * SKEL:(leaf + 1) * SKEL])
        total = nn(skel_potential, interp[leaf]) + near_sum[leaf] + SHIFT * tree_charges[leaf].astype(jnp.float32)
        out[:, leaf * LEAF:(leaf + 1) * LEAF] = total

    for chain in (fx, fy, fyy, *across):
        chain.sent()
    all_of(0, shares, SUBS - 1).wait_send()
    all_of(1, pieces, GROUPS - 1).wait_send()
    all_of(2, whole, SUBS - 1).wait_send()
    all_of(3, near_buf, SUBS - 1).wait_send()


def put_back(tree, order, out):
    total = tree[...]
    high = bf(total)
    rest = total - high.astype(jnp.float32)
    mid = bf(rest)
    low = bf(rest - mid.astype(jnp.float32))
    parts = jnp.concatenate([high, mid, low], axis=0)
    for tile in range(PTS // LEAF):
        take = hot(iota((LEAF, PTS), 0) + tile * LEAF == order[...])
        got = nt(parts, take)
        out[:, tile * LEAF:(tile + 1) * LEAF] = got[:RHS] + got[RHS:2 * RHS] + got[2 * RHS:]


def body(points, charges, leaf_order, near_lists, far_lists, leaf_skeleton, leaf_interp, top_interp, top_skeleton,
         top_owner, top_lists):
    order = leaf_order.reshape(1, PTS)
    near = near_lists.T
    vmem, smem = pl.BlockSpec(memory_space=pltpu.VMEM), pl.BlockSpec(memory_space=pltpu.SMEM)
    shape = jax.ShapeDtypeStruct
    prepared = pl.pallas_call(
        prepare,
        out_shape=(
            shape((LEAVES, DIMS + RHS, SKEL), jnp.bfloat16),
            shape((LEAVES, DIMS + 2 * RHS, SKEL), jnp.bfloat16),
            shape((LEAVES, SKEL, DIMS + 16), jnp.bfloat16),
            shape((LEAVES, LEAF, DIMS + 16), jnp.bfloat16),
            shape((LEAVES, RHS, LEAF), jnp.bfloat16),
            shape((SUBS, 8, 128), jnp.float32),
            shape((16, SUBS * LEAVES), jnp.int32),
        ),
        in_specs=[vmem] * 8,
        out_specs=(vmem,) * 7,
        compiler_params=pltpu.CompilerParams(vmem_limit_bytes=VMEM_LIMIT),
        name="prepare",
    )(points, charges, order, leaf_skeleton, leaf_interp, top_interp, top_skeleton, near)
    *prepared, tables = prepared
    tree = pl.pallas_call(
        main,
        out_shape=shape((RHS, PTS), jnp.float32),
        in_specs=[smem] * 5 + [vmem] * 8,
        out_specs=vmem,
        scratch_shapes=[
            pltpu.VMEM((NX, NY, LEAVES, DIMS + RHS, SKEL), jnp.bfloat16),
            pltpu.VMEM((SUBS, CAP, DIMS + 2 * RHS, SKEL), jnp.bfloat16),
            pltpu.VMEM((SUBS, CAP, DIMS + 2 * RHS, SKEL), jnp.bfloat16),
            pltpu.VMEM((NX, NY, LEAVES, 16, SKEL), jnp.bfloat16),
            pltpu.VMEM((LEAVES, RHS, SKEL), jnp.float32),
            pltpu.VMEM((LEAVES, RHS, LEAF), jnp.float32),
            pltpu.VMEM((SUBS, 8, 128), jnp.float32),
            pltpu.VMEM((8, 128), jnp.float32),
            pltpu.VMEM((GROUPS, 8, 128), jnp.float32),
            pltpu.VMEM((8, 128), jnp.float32),
            pltpu.VMEM((SUBS, 8, 128), jnp.float32),
            pltpu.SemaphoreType.DMA((COPIES,)),
            pltpu.SemaphoreType.DMA((COPIES,)),
            pltpu.SemaphoreType.DMA((4,)),
            pltpu.SemaphoreType.DMA((4,)),
        ],
        compiler_params=pltpu.CompilerParams(
            vmem_limit_bytes=VMEM_LIMIT, collective_id=0, has_side_effects=True),
        name="gather_and_sum",
    )(far_lists, near, top_owner, top_lists.T, tables, *prepared, leaf_interp, top_interp)
    return pl.pallas_call(
        put_back,
        out_shape=shape((RHS, PTS), jnp.float32),
        in_specs=[vmem] * 2,
        out_specs=vmem,
        compiler_params=pltpu.CompilerParams(vmem_limit_bytes=VMEM_LIMIT),
        name="put_back",
    )(tree, order)


def solution(mesh):
    placed = (
        P(None, ("group", "sub")),
        P(None, ("group", "sub")),
        P(("group", "sub")),
        P("group", None),
        P(("group", "sub"), None),
        P(("group", "sub"), None),
        P(("group", "sub"), None, None),
        P("group", "sub"),
        P("group", None),
        P("group"),
        P(),
    )
    return jax.shard_map(
        body, mesh=mesh, in_specs=placed, out_specs=P(None, ("group", "sub")), check_vma=False
    )
```

```python
import functools

import jax
import jax.numpy as jnp
from jax import lax
from jax.experimental import pallas as pl
from jax.experimental.pallas import tpu as pltpu
from jax.sharding import PartitionSpec as P

MESH = pl.DeviceIdType.MESH
DECAY = 3.0**0.5 / 3.0
LOG2E = 1.4426950408889634
TINY = 1e-30
SHIFT = 0.5
DIMS, RHS, LEAF, SKEL, LEAVES, PTS = 32, 16, 256, 128, 8, 2048
NEAR, FAR, TOP, CAP = 7, 80, 256, 2
NX, NY, GROUPS = 4, 8, 16
SUBS = NX * NY
SPLIT = 2
VMEM_LIMIT = 56 << 20


def nn(a, b):
    return lax.dot_general(a, b, (((1,), (0,)), ((), ())), preferred_element_type=jnp.float32)


def nt(a, b):
    return lax.dot_general(a, b, (((1,), (1,)), ((), ())), preferred_element_type=jnp.float32)


def bf(a):
    return a.astype(jnp.bfloat16)


def iota(shape, axis):
    return lax.broadcasted_iota(jnp.int32, shape, axis)


def hot(mask):
    return bf(jnp.where(mask, 1.0, 0.0))


def kernel_values(distance_sq):
    held = jnp.maximum(distance_sq, TINY)
    root = held * lax.rsqrt(held)
    return bf((1.0 + DECAY * root) * jnp.exp2((-DECAY * LOG2E) * root))


def norm_rows(points, first):
    wide = points.astype(jnp.float32)
    norm = jnp.sum(wide * wide, axis=0, keepdims=True)
    high = bf(norm).astype(jnp.float32)
    rest = norm - high
    mid = bf(rest).astype(jnp.float32)
    low = rest - mid
    row = iota((16, points.shape[1]), 0)
    parts = jnp.where(row == first, high, jnp.where(row == first + 1, mid, low))
    ours = (row >= first) & (row < first + 3)
    return bf(jnp.where(ours, parts, jnp.where(row < 6, 1.0, 0.0)))


def target_rows(points, eye):
    stacked = jnp.concatenate([bf(-2.0 * points.astype(jnp.float32)), norm_rows(points, 0)], axis=0)
    return bf(nt(eye, stacked))


def near_tables(near, tables):
    sub = lax.axis_index("sub")
    tables[...] = jnp.zeros_like(tables)
    entries = near[...]
    owner, leaf = entries // LEAVES, lax.rem(entries, LEAVES)
    ours = owner == sub
    least = jnp.min(jnp.where(ours, leaf, LEAVES), axis=0, keepdims=True)
    most = jnp.max(jnp.where(ours, leaf, -1), axis=0, keepdims=True)
    width = SUBS * LEAVES
    for shift in (1, 2, 4):
        least = jnp.minimum(least, pltpu.roll(least, width - shift, 1))
        most = jnp.maximum(most, pltpu.roll(most, width - shift, 1))
    tables[0:1, :] = jnp.where(least < LEAVES, least, 0)
    tables[1:2, :] = jnp.maximum(most, 0)
    mine = pltpu.roll(entries, lax.rem(width - sub * LEAVES, width), 1)[:, :128]
    mine = jnp.where(iota((NEAR, 128), 1) < LEAVES, mine, -1)
    sender = iota((SUBS, 128), 0)
    first = jnp.full((SUBS, 128), LEAVES, jnp.int32)
    rows = []
    for column in range(NEAR):
        row = mine[column:column + 1]
        rows.append((row >> 3 == sender, row & 7, row >> 3))
        first = jnp.minimum(first, jnp.where(rows[-1][0], rows[-1][1], LEAVES))
    first = jnp.min(first, axis=1, keepdims=True)
    for column, (match, leaf, owner) in enumerate(rows):
        lowest = jnp.sum(jnp.where(match, first, 0), axis=0, keepdims=True)
        slot = jnp.where(leaf == lowest, 0, 1)
        tables[2 + column:3 + column, 0:128] = jnp.where(owner >= 0, owner * CAP + slot, 0)


def prepare(points, charges, order, skeleton, interp, send_first, near_pay, tree_points, tree_charges):
    both = jnp.concatenate([points[...], charges[...]], axis=0)
    below = hot(iota((LEAF, LEAF), 1) < iota((LEAF, LEAF), 0))
    ones = jnp.ones((SKEL, SKEL), jnp.bfloat16)
    for leaf in range(LEAVES):
        row = order[:, leaf * LEAF:(leaf + 1) * LEAF]
        mine = bf(nn(both, hot(iota((PTS, LEAF), 0) == row)))
        tree_points[:, leaf * LEAF:(leaf + 1) * LEAF] = mine[:DIMS]
        tree_charges[leaf] = mine[DIMS:]
        chosen = iota((LEAF, SKEL), 0) == skeleton[leaf:leaf + 1, :]
        taken = nn(hot(chosen), ones)
        rank = nn(below, bf(1.0 - taken))
        others = (rank == iota((LEAF, SKEL), 1).astype(jnp.float32)) & (taken == 0.0)
        moved = bf(nn(mine, jnp.concatenate([hot(chosen), hot(others)], axis=1)))
        send_first(leaf, moved[:DIMS, :SKEL], bf(nt(mine[DIMS:], interp[leaf])))
        near_pay[leaf, :DIMS] = moved[:DIMS, SKEL:]
        near_pay[leaf, DIMS:DIMS + RHS] = moved[DIMS:, :SKEL]
        near_pay[leaf, DIMS + RHS:] = moved[DIMS:, SKEL:]


def top_message(pay, tree_points, top_interp, top_skeleton, message):
    eye = hot(iota((TOP, TOP), 0) == iota((TOP, TOP), 1))
    zeros = functools.partial(jnp.zeros, dtype=jnp.bfloat16)
    charges = jnp.concatenate([pay[leaf, DIMS:] for leaf in range(LEAVES)], axis=1)
    count = charges.shape[1]
    spread = jnp.concatenate([charges, zeros((DIMS, count)), charges, zeros((64, count))], axis=0)
    partial = nt(top_interp[...], spread)
    candidate = bf(nn(tree_points[...], hot(iota((PTS, TOP), 0) == top_skeleton[...])))
    placed = nt(eye, jnp.concatenate([zeros((RHS, TOP)), candidate, zeros((128 - RHS - DIMS, TOP))], axis=0))
    high = bf(partial)
    low = bf(partial - high.astype(jnp.float32))
    lane = iota((TOP, 128), 1)
    row = jnp.where(lane < RHS, high.astype(jnp.float32), jnp.where(lane < 48, placed, low.astype(jnp.float32)))
    for peer in range(SUBS):
        message[peer] = bf(row[peer * 8:peer * 8 + 8])


class Chain:
    def __init__(self, buf, sems, base, axis, wide, first, last, turn=0):
        self.buf, self.sems, self.base, self.turn = buf, sems, base, turn
        self.axis, self.wide, self.first, self.last = axis, wide, first, last
        self.n = NY if axis == 1 else NX
        self.steps = self.n // 2
        self.count = 2 * self.steps

    def copy(self, way, step, incoming):
        x, y = lax.axis_index("sub") // NY, lax.rem(lax.axis_index("sub"), NY)
        me = y if self.axis == 1 else x
        sign = 1 if way == 0 else -1
        back = step if incoming else step - 1
        origin = lax.rem(me - sign * back + self.n, self.n)
        to = lax.rem(me + sign + self.n, self.n)
        first, last = self.first, self.last
        if step == self.steps:
            middle = (first + last + 1) // 2
            first, last = (first, middle) if way == 0 else (middle, last)
            if first == last:
                return None
        leaves = pl.ds(first, last - first)
        if self.axis == 1:
            ref = self.buf.at[:, origin, leaves] if self.wide else self.buf.at[x, origin, leaves]
            target = x * NY + to
        else:
            ref = self.buf.at[origin, lax.rem(y + self.turn, NY), leaves]
            target = to * NY + y
        at = self.base + way * self.steps + step - 1
        send, recv = self.sems
        return pltpu.make_async_remote_copy(
            src_ref=ref, dst_ref=ref, send_sem=send.at[at], recv_sem=recv.at[at],
            device_id=(lax.axis_index("group"), target), device_id_type=MESH)

    def each(self, step, incoming):
        return [c for c in (self.copy(way, step, incoming) for way in range(2)) if c is not None]

    def start(self, step):
        for copy in self.each(step, False):
            copy.start()

    def arrive(self, step):
        for copy in self.each(step, True):
            copy.wait_recv()

    def next(self, step):
        for way in range(2):
            self.copy(way, step, True).wait_recv()
            onward = self.copy(way, step + 1, False)
            if onward is not None:
                onward.start()

    def sent(self):
        for step in range(1, self.steps + 1):
            for copy in self.each(step, False):
                copy.wait_send()


COPIES = 2 * NX // 2 + 2 * NY + NY * NX


def main(far_lists, near_lists, top_owner, top_lists,
         points, charges, order, skeleton, near_rows, interp, top_interp, top_skeleton,
         out,
         far_buf, near_out, near_buf, rows_buf, near_pay, far_targets, near_targets, tree_points, tree_charges, message,
         far_sum, near_sum, shares, mine_top, pieces, packed, whole, table_rows, tables,
         send, recv, side_send, side_recv, table_sem):
    sub, group = lax.axis_index("sub"), lax.axis_index("group")
    x, y = sub // NY, lax.rem(sub, NY)

    barrier = pltpu.get_barrier_semaphore()

    def greet_sub(j, carry):
        pl.semaphore_signal(barrier, inc=1, device_id=(group, lax.rem(sub + j, SUBS)), device_id_type=MESH)
        return carry

    def greet_group(j, carry):
        pl.semaphore_signal(barrier, inc=1, device_id=(lax.rem(group + j, GROUPS), sub), device_id_type=MESH)
        return carry

    lax.fori_loop(1, SUBS, greet_sub, 0)
    lax.fori_loop(1, GROUPS, greet_group, 0)

    def send_first(leaf, skel_points, skel_charge):
        far_buf[x, y, leaf, :DIMS] = skel_points
        far_buf[x, y, leaf, DIMS:] = skel_charge

    prepare(points, charges, order, skeleton, interp, send_first, near_pay, tree_points, tree_charges)
    pl.semaphore_wait(barrier, SUBS + GROUPS - 2)

    sems = (send, recv)
    fx = Chain(far_buf, sems, 0, 0, False, 0, SPLIT)
    fy = Chain(far_buf, sems, fx.count, 1, False, SPLIT, LEAVES)
    fyy = Chain(far_buf, sems, fx.count + fy.count, 1, True, 0, SPLIT)
    base = fx.count + fy.count + fyy.count
    across = [Chain(far_buf, sems, base + turn * NX, 0, False, SPLIT, LEAVES, turn) for turn in range(NY)]

    def across_start(*turns):
        for turn in turns:
            across[turn].start(1)

    def across_next(*turns):
        for turn in turns:
            across[turn].next(1)

    def to_sub(level, src, dst):
        def go(j, carry):
            peer = lax.rem(sub + j, SUBS)
            pltpu.make_async_remote_copy(
                src_ref=src(peer), dst_ref=dst.at[sub], send_sem=side_send.at[level], recv_sem=side_recv.at[level],
                device_id=(group, peer), device_id_type=MESH).start()
            return carry
        lax.fori_loop(1, SUBS, go, 0)

    def all_of(level, dst, count):
        ref = dst.at[pl.ds(0, count)]
        return pltpu.make_async_remote_copy(
            src_ref=ref, dst_ref=ref, send_sem=side_send.at[level], recv_sem=side_recv.at[level],
            device_id=(group, lax.rem(sub + 1, SUBS)), device_id_type=MESH)

    lane = iota((8, 128), 1)

    def top_first():
        to_sub(0, lambda peer: message.at[peer], shares)

    def top_second():
        all_of(0, shares, SUBS - 1).wait_recv()
        total = shares[0].astype(jnp.float32)
        for peer in range(1, SUBS):
            total = total + shares[peer].astype(jnp.float32)
        total = total + pltpu.roll(total, 128 - 48, 1)
        chosen = shares[top_owner[0]].astype(jnp.float32)
        chunk = bf(jnp.where(lane < RHS, total, chosen))
        mine_top[...] = chunk
        pieces[group] = chunk

        def go(j, carry):
            pltpu.make_async_remote_copy(
                src_ref=mine_top, dst_ref=pieces.at[group], send_sem=side_send.at[1], recv_sem=side_recv.at[1],
                device_id=(lax.rem(group + j, GROUPS), sub), device_id_type=MESH).start()
            return carry
        lax.fori_loop(1, GROUPS, go, 0)

    def top_third():
        all_of(1, pieces, GROUPS - 1).wait_recv()
        one = pieces[top_lists[0, group]].astype(jnp.float32)
        two = pieces[top_lists[1, group]].astype(jnp.float32)
        mine = mine_top[...].astype(jnp.float32)
        row = bf(jnp.where(lane < 48, one, jnp.where(lane < 96, pltpu.roll(two, 48, 1), pltpu.roll(mine, 80, 1))))
        packed[...] = row
        whole[sub] = row
        to_sub(2, lambda peer: packed, whole)

    fx.start(1)
    fy.start(1)
    across_start(0)
    top_message(far_buf.at[x, y], tree_points, top_interp, top_skeleton, message)
    shares[sub] = message[sub]
    fx.next(1)
    top_first()
    fy.next(1)
    across_start(1, NY - 1)
    fx.arrive(2)
    fyy.start(1)
    near_tables(near_rows, table_rows)
    fetch = pltpu.make_async_copy(table_rows, tables, table_sem)
    fetch.start()
    across_next(0)
    eye = hot(iota((LEAF, LEAF), 0) == iota((LEAF, LEAF), 1))
    for leaf in range(LEAVES):
        far_targets[leaf] = target_rows(far_buf[x, y, leaf, :DIMS], eye[:SKEL, :SKEL])
    fy.next(2)
    across_start(2, NY - 2)
    fetch.wait()

    def pick_near(peer, carry):
        for slot in range(CAP):
            near_out[peer, slot] = near_pay[tables[slot, peer * LEAVES]]
        return carry

    lax.fori_loop(0, SUBS, pick_near, 0)
    fyy.next(1)
    across_next(1, NY - 1)
    fy.next(3)
    across_start(3, NY - 3)
    for leaf in range(LEAVES):
        near_targets[leaf] = target_rows(tree_points[:, leaf * LEAF:(leaf + 1) * LEAF], eye)
    top_second()
    fyy.next(2)
    fy.arrive(4)
    across_start(4)
    across_next(2, NY - 2)
    fyy.next(3)
    to_sub(3, lambda peer: near_out.at[peer], near_buf)
    across_next(3, NY - 3)
    top_third()
    across_next(4)
    fyy.arrive(4)
    for turn in range(NY):
        across[turn].arrive(2)

    def fill_rows(dev, carry):
        for leaf in range(LEAVES):
            rows_buf[dev // NY, lax.rem(dev, NY), leaf] = norm_rows(
                far_buf[dev // NY, lax.rem(dev, NY), leaf, :DIMS], 3)
        return carry

    lax.fori_loop(0, SUBS, fill_rows, 0)

    def place(index):
        return index // (NY * LEAVES), lax.rem(index // LEAVES, NY), lax.rem(index, LEAVES)

    def far_leaf(leaf, carry):
        sources, charges = [], []
        for entry in range(FAR):
            a, b, c = place(far_lists[leaf, entry])
            got = far_buf[a, b, c]
            sources.append(jnp.concatenate([got[:DIMS], rows_buf[a, b, c]], axis=0))
            charges.append(got[DIMS:])
        values = kernel_values(nn(far_targets[leaf], jnp.concatenate(sources, axis=1)))
        far_sum[leaf] = nt(jnp.concatenate(charges, axis=1), values)
        return carry

    lax.fori_loop(0, LEAVES, far_leaf, 0)
    all_of(3, near_buf, SUBS - 1).wait_recv()

    def near_leaf(leaf, carry):
        sources, charges = [], []
        for entry in range(NEAR + 1):
            if entry == 0:
                a, b, c = x, y, leaf
                got = near_pay[leaf]
            else:
                a, b, c = place(near_lists[entry - 1, sub * LEAVES + leaf])
                at = tables[entry + 1, leaf]
                got = near_buf[at // CAP, lax.rem(at, CAP)]
            sources.append(jnp.concatenate([far_buf[a, b, c, :DIMS], rows_buf[a, b, c]], axis=0))
            sources.append(jnp.concatenate([got[:DIMS], norm_rows(got[:DIMS], 3)], axis=0))
            charges.append(got[DIMS:DIMS + RHS])
            charges.append(got[DIMS + RHS:])
        values = kernel_values(nn(near_targets[leaf], jnp.concatenate(sources, axis=1)))
        near_sum[leaf] = nt(jnp.concatenate(charges, axis=1), values)
        return carry

    lax.fori_loop(0, LEAVES, near_leaf, 0)

    all_of(2, whole, SUBS - 1).wait_recv()
    table = jnp.concatenate([whole[peer].astype(jnp.float32) for peer in range(SUBS)], axis=0)
    narrow = bf(table)
    lanes = iota((TOP, 128), 1)
    squares = table * table
    square_high = bf(squares)
    square_low = bf(squares - square_high.astype(jnp.float32))
    own_norm = jnp.sum(jnp.where(lanes >= 96, squares, 0.0), axis=1, keepdims=True)
    potential = jnp.zeros((RHS, TOP), jnp.float32)
    for which in range(2):
        start = 48 * which
        points_at = (lanes >= start + RHS) & (lanes < start + 48)
        aligned = pltpu.roll(table, (start + RHS - 96) % 128, 1)
        left = bf(jnp.where(points_at, -2.0 * aligned, 0.0))
        flags = hot((iota((8, 128), 1) >= start + RHS) & (iota((8, 128), 1) < start + 48))
        other_norm = nt(flags, square_high) + nt(flags, square_low)
        values = kernel_values(nt(left, narrow) + own_norm + other_norm[:1])
        pick = hot(iota((RHS, 128), 1) == iota((RHS, 128), 0) + start)
        potential = potential + nt(bf(nt(pick, narrow)), values)
    down = nn(bf(potential), top_interp[...])

    for leaf in range(LEAVES):
        skel_potential = bf(far_sum[leaf] + down[:, leaf * SKEL:(leaf + 1) * SKEL])
        total = nn(skel_potential, interp[leaf]) + near_sum[leaf] + SHIFT * tree_charges[leaf].astype(jnp.float32)
        out[:, leaf * LEAF:(leaf + 1) * LEAF] = total

    for chain in (fx, fy, fyy, *across):
        chain.sent()
    all_of(0, shares, SUBS - 1).wait_send()
    all_of(1, pieces, GROUPS - 1).wait_send()
    all_of(2, whole, SUBS - 1).wait_send()
    all_of(3, near_buf, SUBS - 1).wait_send()


def put_back(tree, order, out):
    total = tree[...]
    high = bf(total)
    rest = total - high.astype(jnp.float32)
    mid = bf(rest)
    low = bf(rest - mid.astype(jnp.float32))
    parts = jnp.concatenate([high, mid, low], axis=0)
    for tile in range(PTS // LEAF):
        take = hot(iota((LEAF, PTS), 0) + tile * LEAF == order[...])
        got = nt(parts, take)
        out[:, tile * LEAF:(tile + 1) * LEAF] = got[:RHS] + got[RHS:2 * RHS] + got[2 * RHS:]


def body(points, charges, leaf_order, near_lists, far_lists, leaf_skeleton, leaf_interp, top_interp, top_skeleton,
         top_owner, top_lists):
    order = leaf_order.reshape(1, PTS)
    near = near_lists.T
    vmem, smem = pl.BlockSpec(memory_space=pltpu.VMEM), pl.BlockSpec(memory_space=pltpu.SMEM)
    shape = jax.ShapeDtypeStruct
    tree = pl.pallas_call(
        main,
        out_shape=shape((RHS, PTS), jnp.float32),
        in_specs=[smem] * 4 + [vmem] * 8,
        out_specs=vmem,
        scratch_shapes=[
            pltpu.VMEM((NX, NY, LEAVES, DIMS + RHS, SKEL), jnp.bfloat16),
            pltpu.VMEM((SUBS, CAP, DIMS + 2 * RHS, SKEL), jnp.bfloat16),
            pltpu.VMEM((SUBS, CAP, DIMS + 2 * RHS, SKEL), jnp.bfloat16),
            pltpu.VMEM((NX, NY, LEAVES, 16, SKEL), jnp.bfloat16),
            pltpu.VMEM((LEAVES, DIMS + 2 * RHS, SKEL), jnp.bfloat16),
            pltpu.VMEM((LEAVES, SKEL, DIMS + 16), jnp.bfloat16),
            pltpu.VMEM((LEAVES, LEAF, DIMS + 16), jnp.bfloat16),
            pltpu.VMEM((DIMS, PTS), jnp.bfloat16),
            pltpu.VMEM((LEAVES, RHS, LEAF), jnp.bfloat16),
            pltpu.VMEM((SUBS, 8, 128), jnp.bfloat16),
            pltpu.VMEM((LEAVES, RHS, SKEL), jnp.float32),
            pltpu.VMEM((LEAVES, RHS, LEAF), jnp.float32),
            pltpu.VMEM((SUBS, 8, 128), jnp.bfloat16),
            pltpu.VMEM((8, 128), jnp.bfloat16),
            pltpu.VMEM((GROUPS, 8, 128), jnp.bfloat16),
            pltpu.VMEM((8, 128), jnp.bfloat16),
            pltpu.VMEM((SUBS, 8, 128), jnp.bfloat16),
            pltpu.VMEM((16, SUBS * LEAVES), jnp.int32),
            pltpu.SMEM((16, SUBS * LEAVES), jnp.int32),
            pltpu.SemaphoreType.DMA((COPIES,)),
            pltpu.SemaphoreType.DMA((COPIES,)),
            pltpu.SemaphoreType.DMA((4,)),
            pltpu.SemaphoreType.DMA((4,)),
            pltpu.SemaphoreType.DMA,
        ],
        compiler_params=pltpu.CompilerParams(
            vmem_limit_bytes=VMEM_LIMIT, collective_id=0, has_side_effects=True),
        name="gather_and_sum",
    )(far_lists, near, top_owner, top_lists.T, points, charges, order, leaf_skeleton, near, leaf_interp, top_interp,
      top_skeleton)
    return pl.pallas_call(
        put_back,
        out_shape=shape((RHS, PTS), jnp.float32),
        in_specs=[vmem] * 2,
        out_specs=vmem,
        compiler_params=pltpu.CompilerParams(vmem_limit_bytes=VMEM_LIMIT),
        name="put_back",
    )(tree, order)


def solution(mesh):
    placed = (
        P(None, ("group", "sub")),
        P(None, ("group", "sub")),
        P(("group", "sub")),
        P("group", None),
        P(("group", "sub"), None),
        P(("group", "sub"), None),
        P(("group", "sub"), None, None),
        P("group", "sub"),
        P("group", None),
        P("group"),
        P(),
    )
    return jax.shard_map(
        body, mesh=mesh, in_specs=placed, out_specs=P(None, ("group", "sub")), check_vma=False
    )
```

```python
import functools

import jax
import jax.numpy as jnp
from jax import lax
from jax.experimental import pallas as pl
from jax.experimental.pallas import tpu as pltpu
from jax.sharding import PartitionSpec as P

MESH = pl.DeviceIdType.MESH
DECAY = 3.0**0.5 / 3.0
LOG2E = 1.4426950408889634
TINY = 1e-30
SHIFT = 0.5
DIMS, RHS, LEAF, SKEL, LEAVES, PTS = 32, 16, 256, 128, 8, 2048
NEAR, FAR, TOP, CAP = 7, 80, 256, 2
NX, NY, GROUPS = 4, 8, 16
SUBS = NX * NY
SPLIT = 2
VMEM_LIMIT = 56 << 20


def nn(a, b):
    return lax.dot_general(a, b, (((1,), (0,)), ((), ())), preferred_element_type=jnp.float32)


def nt(a, b):
    return lax.dot_general(a, b, (((1,), (1,)), ((), ())), preferred_element_type=jnp.float32)


def bf(a):
    return a.astype(jnp.bfloat16)


def iota(shape, axis):
    return lax.broadcasted_iota(jnp.int32, shape, axis)


def hot(mask):
    return bf(jnp.where(mask, 1.0, 0.0))


def kernel_values(distance_sq):
    held = jnp.maximum(distance_sq, TINY)
    root = held * lax.rsqrt(held)
    return bf((1.0 + DECAY * root) * jnp.exp2((-DECAY * LOG2E) * root))


def norm_rows(points, first):
    wide = points.astype(jnp.float32)
    norm = jnp.sum(wide * wide, axis=0, keepdims=True)
    high = bf(norm).astype(jnp.float32)
    rest = norm - high
    mid = bf(rest).astype(jnp.float32)
    low = rest - mid
    row = iota((16, points.shape[1]), 0)
    parts = jnp.where(row == first, high, jnp.where(row == first + 1, mid, low))
    ours = (row >= first) & (row < first + 3)
    return bf(jnp.where(ours, parts, jnp.where(row < 6, 1.0, 0.0)))


def target_rows(points, eye):
    stacked = jnp.concatenate([bf(-2.0 * points.astype(jnp.float32)), norm_rows(points, 0)], axis=0)
    return bf(nt(eye, stacked))


def near_tables(near, tables):
    sub = lax.axis_index("sub")
    tables[...] = jnp.zeros_like(tables)
    entries = near[...]
    owner, leaf = entries // LEAVES, lax.rem(entries, LEAVES)
    ours = owner == sub
    least = jnp.min(jnp.where(ours, leaf, LEAVES), axis=0, keepdims=True)
    most = jnp.max(jnp.where(ours, leaf, -1), axis=0, keepdims=True)
    width = SUBS * LEAVES
    for shift in (1, 2, 4):
        least = jnp.minimum(least, pltpu.roll(least, width - shift, 1))
        most = jnp.maximum(most, pltpu.roll(most, width - shift, 1))
    tables[0:1, :] = jnp.where(least < LEAVES, least, 0)
    tables[1:2, :] = jnp.maximum(most, 0)
    mine = pltpu.roll(entries, lax.rem(width - sub * LEAVES, width), 1)[:, :128]
    mine = jnp.where(iota((NEAR, 128), 1) < LEAVES, mine, -1)
    sender = iota((SUBS, 128), 0)
    first = jnp.full((SUBS, 128), LEAVES, jnp.int32)
    rows = []
    for column in range(NEAR):
        row = mine[column:column + 1]
        rows.append((row >> 3 == sender, row & 7, row >> 3))
        first = jnp.minimum(first, jnp.where(rows[-1][0], rows[-1][1], LEAVES))
    first = jnp.min(first, axis=1, keepdims=True)
    for column, (match, leaf, owner) in enumerate(rows):
        lowest = jnp.sum(jnp.where(match, first, 0), axis=0, keepdims=True)
        slot = jnp.where(leaf == lowest, 0, 1)
        tables[2 + column:3 + column, 0:128] = jnp.where(owner >= 0, owner * CAP + slot, 0)


def prepare(points, charges, order, skeleton, interp, send_first, near_skel, near_rest, tree_points, tree_charges):
    both = jnp.concatenate([points[...], charges[...]], axis=0)
    below = hot(iota((LEAF, LEAF), 1) < iota((LEAF, LEAF), 0))
    ones = jnp.ones((SKEL, SKEL), jnp.bfloat16)
    for leaf in range(LEAVES):
        row = order[:, leaf * LEAF:(leaf + 1) * LEAF]
        mine = bf(nn(both, hot(iota((PTS, LEAF), 0) == row)))
        tree_points[:, leaf * LEAF:(leaf + 1) * LEAF] = mine[:DIMS]
        tree_charges[leaf] = mine[DIMS:]
        chosen = iota((LEAF, SKEL), 0) == skeleton[leaf:leaf + 1, :]
        taken = nn(hot(chosen), ones)
        rank = nn(below, bf(1.0 - taken))
        others = (rank == iota((LEAF, SKEL), 1).astype(jnp.float32)) & (taken == 0.0)
        moved = bf(nn(mine, jnp.concatenate([hot(chosen), hot(others)], axis=1)))
        send_first(leaf, moved[:DIMS, :SKEL], bf(nt(mine[DIMS:], interp[leaf])))
        near_skel[leaf] = moved[DIMS:, :SKEL]
        near_rest[leaf] = moved[:, SKEL:]


def top_message(pay, tree_points, top_interp, top_skeleton, message):
    eye = hot(iota((TOP, TOP), 0) == iota((TOP, TOP), 1))
    zeros = functools.partial(jnp.zeros, dtype=jnp.bfloat16)
    charges = jnp.concatenate([pay[leaf, DIMS:] for leaf in range(LEAVES)], axis=1)
    count = charges.shape[1]
    spread = jnp.concatenate([charges, zeros((DIMS, count)), charges, zeros((64, count))], axis=0)
    partial = nt(top_interp[...], spread)
    candidate = bf(nn(tree_points[...], hot(iota((PTS, TOP), 0) == top_skeleton[...])))
    placed = nt(eye, jnp.concatenate([zeros((RHS, TOP)), candidate, zeros((128 - RHS - DIMS, TOP))], axis=0))
    high = bf(partial)
    low = bf(partial - high.astype(jnp.float32))
    lane = iota((TOP, 128), 1)
    row = jnp.where(lane < RHS, high.astype(jnp.float32), jnp.where(lane < 48, placed, low.astype(jnp.float32)))
    for peer in range(SUBS):
        message[peer] = bf(row[peer * 8:peer * 8 + 8])


class Chain:
    def __init__(self, buf, sems, base, axis, wide, first, last, turn=0):
        self.buf, self.sems, self.base, self.turn = buf, sems, base, turn
        self.axis, self.wide, self.first, self.last = axis, wide, first, last
        self.n = NY if axis == 1 else NX
        self.steps = self.n // 2
        self.count = 2 * self.steps

    def copy(self, way, step, incoming):
        x, y = lax.axis_index("sub") // NY, lax.rem(lax.axis_index("sub"), NY)
        me = y if self.axis == 1 else x
        sign = 1 if way == 0 else -1
        back = step if incoming else step - 1
        origin = lax.rem(me - sign * back + self.n, self.n)
        to = lax.rem(me + sign + self.n, self.n)
        first, last = self.first, self.last
        if step == self.steps:
            middle = (first + last + 1) // 2
            first, last = (first, middle) if way == 0 else (middle, last)
            if first == last:
                return None
        leaves = pl.ds(first, last - first)
        if self.axis == 1:
            ref = self.buf.at[:, origin, leaves] if self.wide else self.buf.at[x, origin, leaves]
            target = x * NY + to
        else:
            ref = self.buf.at[origin, lax.rem(y + self.turn, NY), leaves]
            target = to * NY + y
        at = self.base + way * self.steps + step - 1
        send, recv = self.sems
        return pltpu.make_async_remote_copy(
            src_ref=ref, dst_ref=ref, send_sem=send.at[at], recv_sem=recv.at[at],
            device_id=(lax.axis_index("group"), target), device_id_type=MESH)

    def each(self, step, incoming):
        return [c for c in (self.copy(way, step, incoming) for way in range(2)) if c is not None]

    def start(self, step):
        for copy in self.each(step, False):
            copy.start()

    def arrive(self, step):
        for copy in self.each(step, True):
            copy.wait_recv()

    def next(self, step):
        for way in range(2):
            self.copy(way, step, True).wait_recv()
            onward = self.copy(way, step + 1, False)
            if onward is not None:
                onward.start()

    def sent(self):
        for step in range(1, self.steps + 1):
            for copy in self.each(step, False):
                copy.wait_send()


COPIES = 2 * NX // 2 + 2 * NY + NY * NX


def main(far_lists, near_lists, top_owner, top_lists,
         points, charges, order, skeleton, near_rows, interp, top_interp, top_skeleton,
         out, inverse,
         far_buf, skel_out, skel_buf, rest_out, rest_buf, rows_buf, near_skel, near_rest, far_targets, near_targets, tree_points, tree_charges, message,
         far_sum, near_sum, shares, mine_top, pieces, packed, whole, table_rows, tables,
         send, recv, side_send, side_recv, table_sem):
    sub, group = lax.axis_index("sub"), lax.axis_index("group")
    x, y = sub // NY, lax.rem(sub, NY)

    barrier = pltpu.get_barrier_semaphore()

    def greet_sub(j, carry):
        pl.semaphore_signal(barrier, inc=1, device_id=(group, lax.rem(sub + j, SUBS)), device_id_type=MESH)
        return carry

    def greet_group(j, carry):
        pl.semaphore_signal(barrier, inc=1, device_id=(lax.rem(group + j, GROUPS), sub), device_id_type=MESH)
        return carry

    lax.fori_loop(1, SUBS, greet_sub, 0)
    lax.fori_loop(1, GROUPS, greet_group, 0)

    def send_first(leaf, skel_points, skel_charge):
        far_buf[x, y, leaf, :DIMS] = skel_points
        far_buf[x, y, leaf, DIMS:] = skel_charge

    prepare(points, charges, order, skeleton, interp, send_first, near_skel, near_rest, tree_points, tree_charges)
    pl.semaphore_wait(barrier, SUBS + GROUPS - 2)

    sems = (send, recv)
    fx = Chain(far_buf, sems, 0, 0, False, 0, SPLIT)
    fy = Chain(far_buf, sems, fx.count, 1, False, SPLIT, LEAVES)
    fyy = Chain(far_buf, sems, fx.count + fy.count, 1, True, 0, SPLIT)
    base = fx.count + fy.count + fyy.count
    across = [Chain(far_buf, sems, base + turn * NX, 0, False, SPLIT, LEAVES, turn) for turn in range(NY)]

    def across_start(*turns):
        for turn in turns:
            across[turn].start(1)

    def across_next(*turns):
        for turn in turns:
            across[turn].next(1)

    def to_sub(level, src, dst):
        def go(j, carry):
            peer = lax.rem(sub + j, SUBS)
            pltpu.make_async_remote_copy(
                src_ref=src(peer), dst_ref=dst.at[sub], send_sem=side_send.at[level], recv_sem=side_recv.at[level],
                device_id=(group, peer), device_id_type=MESH).start()
            return carry
        lax.fori_loop(1, SUBS, go, 0)

    def all_of(level, dst, count):
        ref = dst.at[pl.ds(0, count)]
        return pltpu.make_async_remote_copy(
            src_ref=ref, dst_ref=ref, send_sem=side_send.at[level], recv_sem=side_recv.at[level],
            device_id=(group, lax.rem(sub + 1, SUBS)), device_id_type=MESH)

    lane = iota((8, 128), 1)

    def top_first():
        to_sub(0, lambda peer: message.at[peer], shares)

    def top_second():
        all_of(0, shares, SUBS - 1).wait_recv()
        total = shares[0].astype(jnp.float32)
        for peer in range(1, SUBS):
            total = total + shares[peer].astype(jnp.float32)
        total = total + pltpu.roll(total, 128 - 48, 1)
        chosen = shares[top_owner[0]].astype(jnp.float32)
        chunk = bf(jnp.where(lane < RHS, total, chosen))
        mine_top[...] = chunk
        pieces[group] = chunk

        def go(j, carry):
            pltpu.make_async_remote_copy(
                src_ref=mine_top, dst_ref=pieces.at[group], send_sem=side_send.at[1], recv_sem=side_recv.at[1],
                device_id=(lax.rem(group + j, GROUPS), sub), device_id_type=MESH).start()
            return carry
        lax.fori_loop(1, GROUPS, go, 0)

    def top_third():
        all_of(1, pieces, GROUPS - 1).wait_recv()
        one = pieces[top_lists[0, group]].astype(jnp.float32)
        two = pieces[top_lists[1, group]].astype(jnp.float32)
        mine = mine_top[...].astype(jnp.float32)
        row = bf(jnp.where(lane < 48, one, jnp.where(lane < 96, pltpu.roll(two, 48, 1), pltpu.roll(mine, 80, 1))))
        packed[...] = row
        whole[sub] = row
        to_sub(2, lambda peer: packed, whole)

    fx.start(1)
    fy.start(1)
    across_start(0)
    top_message(far_buf.at[x, y], tree_points, top_interp, top_skeleton, message)
    shares[sub] = message[sub]
    fx.next(1)
    top_first()
    fy.next(1)
    across_start(1, NY - 1)
    fx.arrive(2)
    fyy.start(1)
    near_tables(near_rows, table_rows)
    fetch = pltpu.make_async_copy(table_rows, tables, table_sem)
    fetch.start()
    across_next(0)
    eye = hot(iota((LEAF, LEAF), 0) == iota((LEAF, LEAF), 1))
    for leaf in range(LEAVES):
        far_targets[leaf] = target_rows(far_buf[x, y, leaf, :DIMS], eye[:SKEL, :SKEL])
    fy.next(2)
    across_start(2, NY - 2)
    fetch.wait()

    def pick_near(peer, carry):
        for slot in range(CAP):
            leaf = tables[slot, peer * LEAVES]
            skel_out[peer, slot] = near_skel[leaf]
            rest_out[peer, slot] = near_rest[leaf]
        return carry

    lax.fori_loop(0, SUBS, pick_near, 0)
    fyy.next(1)
    across_next(1, NY - 1)
    fy.next(3)
    across_start(3, NY - 3)
    for leaf in range(LEAVES):
        near_targets[leaf] = target_rows(tree_points[:, leaf * LEAF:(leaf + 1) * LEAF], eye)
    top_second()
    fyy.next(2)
    at = iota((16, PTS), 1)
    digits = bf(jnp.where(iota((16, PTS), 0) == 0, at >> 8, at & 255).astype(jnp.float32))
    for tile in range(PTS // LEAF):
        got = nt(digits, hot(iota((LEAF, PTS), 0) + tile * LEAF == order[...]))
        row = 256.0 * got[0:1] + got[1:2]
        inverse[:, tile * LEAF:(tile + 1) * LEAF] = jnp.broadcast_to(row, (8, LEAF)).astype(jnp.int32)
    fy.arrive(4)
    across_start(4)
    across_next(2, NY - 2)
    fyy.next(3)
    across_next(3, NY - 3)
    top_third()
    across_next(4)
    to_sub(3, lambda peer: skel_out.at[peer], skel_buf)
    to_sub(4, lambda peer: rest_out.at[peer], rest_buf)
    fyy.arrive(4)
    for turn in range(NY):
        across[turn].arrive(2)

    def fill_rows(dev, carry):
        for leaf in range(LEAVES):
            rows_buf[dev // NY, lax.rem(dev, NY), leaf] = norm_rows(
                far_buf[dev // NY, lax.rem(dev, NY), leaf, :DIMS], 3)
        return carry

    lax.fori_loop(0, SUBS, fill_rows, 0)

    def place(index):
        return index >> 6, (index >> 3) & 7, index & 7

    def far_leaf(leaf, carry):
        sources, charges = [], []
        for entry in range(FAR):
            a, b, c = place(far_lists[leaf, entry])
            got = far_buf[a, b, c]
            sources.append(jnp.concatenate([got[:DIMS], rows_buf[a, b, c]], axis=0))
            charges.append(got[DIMS:])
        values = kernel_values(nn(far_targets[leaf], jnp.concatenate(sources, axis=1)))
        far_sum[leaf] = nt(jnp.concatenate(charges, axis=1), values)
        return carry

    lax.fori_loop(0, LEAVES, far_leaf, 0)
    def near_pass(leaf, points_of, charges_of):
        sources, charges = [], []
        for entry in range(NEAR + 1):
            if entry == 0:
                where, at = (x, y, leaf), None
            else:
                where = place(near_lists[entry - 1, sub * LEAVES + leaf])
                at = tables[entry + 1, leaf]
            sources.append(points_of(where, at, leaf))
            charges.append(charges_of(at, leaf))
        values = kernel_values(nn(near_targets[leaf], jnp.concatenate(sources, axis=1)))
        return nt(jnp.concatenate(charges, axis=1), values)

    def slot_of(at):
        return at >> 1, at & 1

    def near_first(leaf, carry):
        def points_of(where, at, leaf):
            return jnp.concatenate([far_buf[(*where, slice(0, DIMS))], rows_buf[where]], axis=0)

        def charges_of(at, leaf):
            return near_skel[leaf] if at is None else skel_buf[slot_of(at)]

        near_sum[leaf] = near_pass(leaf, points_of, charges_of)
        return carry

    def near_second(leaf, carry):
        def both_of(at, leaf):
            return near_rest[leaf] if at is None else rest_buf[slot_of(at)]

        def points_of(where, at, leaf):
            points = both_of(at, leaf)[:DIMS]
            return jnp.concatenate([points, norm_rows(points, 3)], axis=0)

        near_sum[leaf] = near_sum[leaf] + near_pass(leaf, points_of, lambda at, leaf: both_of(at, leaf)[DIMS:])
        return carry

    all_of(3, skel_buf, SUBS - 1).wait_recv()
    lax.fori_loop(0, LEAVES, near_first, 0)
    all_of(4, rest_buf, SUBS - 1).wait_recv()
    lax.fori_loop(0, LEAVES, near_second, 0)

    all_of(2, whole, SUBS - 1).wait_recv()
    table = jnp.concatenate([whole[peer].astype(jnp.float32) for peer in range(SUBS)], axis=0)
    narrow = bf(table)
    lanes = iota((TOP, 128), 1)
    squares = table * table
    square_high = bf(squares)
    square_low = bf(squares - square_high.astype(jnp.float32))
    own_norm = jnp.sum(jnp.where(lanes >= 96, squares, 0.0), axis=1, keepdims=True)
    potential = jnp.zeros((RHS, TOP), jnp.float32)
    for which in range(2):
        start = 48 * which
        points_at = (lanes >= start + RHS) & (lanes < start + 48)
        aligned = pltpu.roll(table, (start + RHS - 96) % 128, 1)
        left = bf(jnp.where(points_at, -2.0 * aligned, 0.0))
        flags = hot((iota((8, 128), 1) >= start + RHS) & (iota((8, 128), 1) < start + 48))
        other_norm = nt(flags, square_high) + nt(flags, square_low)
        values = kernel_values(nt(left, narrow) + own_norm + other_norm[:1])
        pick = hot(iota((RHS, 128), 1) == iota((RHS, 128), 0) + start)
        potential = potential + nt(bf(nt(pick, narrow)), values)
    down = nn(bf(potential), top_interp[...])

    for leaf in range(LEAVES):
        skel_potential = bf(far_sum[leaf] + down[:, leaf * SKEL:(leaf + 1) * SKEL])
        total = nn(skel_potential, interp[leaf]) + near_sum[leaf] + SHIFT * tree_charges[leaf].astype(jnp.float32)
        out[:, leaf * LEAF:(leaf + 1) * LEAF] = total

    for chain in (fx, fy, fyy, *across):
        chain.sent()
    all_of(0, shares, SUBS - 1).wait_send()
    all_of(1, pieces, GROUPS - 1).wait_send()
    all_of(2, whole, SUBS - 1).wait_send()
    all_of(3, skel_buf, SUBS - 1).wait_send()
    all_of(4, rest_buf, SUBS - 1).wait_send()


def put_back(tree, inverse, out):
    for tile in range(PTS // 128):
        lanes = pl.ds(tile * 128, 128)
        column = inverse[:, lanes]
        within, block = column & 127, column >> 7
        for half in range(RHS // 8):
            rows = pl.ds(half * 8, 8)
            got = jnp.zeros((8, 128), jnp.float32)
            for source in range(PTS // 128):
                moved = jnp.take_along_axis(tree[rows, pl.ds(source * 128, 128)], within, axis=1,
                                            mode="promise_in_bounds")
                got = jnp.where(block == source, moved, got)
            out[rows, lanes] = got


def body(points, charges, leaf_order, near_lists, far_lists, leaf_skeleton, leaf_interp, top_interp, top_skeleton,
         top_owner, top_lists):
    order = leaf_order.reshape(1, PTS)
    near = near_lists.T
    vmem, smem = pl.BlockSpec(memory_space=pltpu.VMEM), pl.BlockSpec(memory_space=pltpu.SMEM)
    shape = jax.ShapeDtypeStruct
    tree, inverse = pl.pallas_call(
        main,
        out_shape=(shape((RHS, PTS), jnp.float32), shape((8, PTS), jnp.int32)),
        in_specs=[smem] * 4 + [vmem] * 8,
        out_specs=(vmem, vmem),
        scratch_shapes=[
            pltpu.VMEM((NX, NY, LEAVES, DIMS + RHS, SKEL), jnp.bfloat16),
            pltpu.VMEM((SUBS, CAP, RHS, SKEL), jnp.bfloat16),
            pltpu.VMEM((SUBS, CAP, RHS, SKEL), jnp.bfloat16),
            pltpu.VMEM((SUBS, CAP, DIMS + RHS, SKEL), jnp.bfloat16),
            pltpu.VMEM((SUBS, CAP, DIMS + RHS, SKEL), jnp.bfloat16),
            pltpu.VMEM((NX, NY, LEAVES, 16, SKEL), jnp.bfloat16),
            pltpu.VMEM((LEAVES, RHS, SKEL), jnp.bfloat16),
            pltpu.VMEM((LEAVES, DIMS + RHS, SKEL), jnp.bfloat16),
            pltpu.VMEM((LEAVES, SKEL, DIMS + 16), jnp.bfloat16),
            pltpu.VMEM((LEAVES, LEAF, DIMS + 16), jnp.bfloat16),
            pltpu.VMEM((DIMS, PTS), jnp.bfloat16),
            pltpu.VMEM((LEAVES, RHS, LEAF), jnp.bfloat16),
            pltpu.VMEM((SUBS, 8, 128), jnp.bfloat16),
            pltpu.VMEM((LEAVES, RHS, SKEL), jnp.float32),
            pltpu.VMEM((LEAVES, RHS, LEAF), jnp.float32),
            pltpu.VMEM((SUBS, 8, 128), jnp.bfloat16),
            pltpu.VMEM((8, 128), jnp.bfloat16),
            pltpu.VMEM((GROUPS, 8, 128), jnp.bfloat16),
            pltpu.VMEM((8, 128), jnp.bfloat16),
            pltpu.VMEM((SUBS, 8, 128), jnp.bfloat16),
            pltpu.VMEM((16, SUBS * LEAVES), jnp.int32),
            pltpu.SMEM((16, SUBS * LEAVES), jnp.int32),
            pltpu.SemaphoreType.DMA((COPIES,)),
            pltpu.SemaphoreType.DMA((COPIES,)),
            pltpu.SemaphoreType.DMA((5,)),
            pltpu.SemaphoreType.DMA((5,)),
            pltpu.SemaphoreType.DMA,
        ],
        compiler_params=pltpu.CompilerParams(
            vmem_limit_bytes=VMEM_LIMIT, collective_id=0, has_side_effects=True),
        name="gather_and_sum",
    )(far_lists, near, top_owner, top_lists.T, points, charges, order, leaf_skeleton, near, leaf_interp, top_interp,
      top_skeleton)
    return pl.pallas_call(
        put_back,
        out_shape=shape((RHS, PTS), jnp.float32),
        in_specs=[vmem] * 2,
        out_specs=vmem,
        compiler_params=pltpu.CompilerParams(vmem_limit_bytes=VMEM_LIMIT),
        name="put_back",
    )(tree, inverse)


def solution(mesh):
    placed = (
        P(None, ("group", "sub")),
        P(None, ("group", "sub")),
        P(("group", "sub")),
        P("group", None),
        P(("group", "sub"), None),
        P(("group", "sub"), None),
        P(("group", "sub"), None, None),
        P("group", "sub"),
        P("group", None),
        P("group"),
        P(),
    )
    return jax.shard_map(
        body, mesh=mesh, in_specs=placed, out_specs=P(None, ("group", "sub")), check_vma=False
    )
```

```python
import functools

import jax
import jax.numpy as jnp
from jax import lax
from jax.experimental import pallas as pl
from jax.experimental.pallas import tpu as pltpu
from jax.sharding import PartitionSpec as P

MESH = pl.DeviceIdType.MESH
DECAY = 3.0**0.5 / 3.0
LOG2E = 1.4426950408889634
TINY = 1e-30
SHIFT = 0.5
DIMS, RHS, LEAF, SKEL, LEAVES, PTS = 32, 16, 256, 128, 8, 2048
NEAR, FAR, TOP, CAP = 7, 80, 256, 2
NX, NY, GROUPS = 4, 8, 16
SUBS = NX * NY
SPLIT = 2
VMEM_LIMIT = 56 << 20


def nn(a, b):
    return lax.dot_general(a, b, (((1,), (0,)), ((), ())), preferred_element_type=jnp.float32)


def nt(a, b):
    return lax.dot_general(a, b, (((1,), (1,)), ((), ())), preferred_element_type=jnp.float32)


def bf(a):
    return a.astype(jnp.bfloat16)


def iota(shape, axis):
    return lax.broadcasted_iota(jnp.int32, shape, axis)


def hot(mask):
    return bf(jnp.where(mask, 1.0, 0.0))


def kernel_values(distance_sq):
    held = jnp.maximum(distance_sq, TINY)
    root = held * lax.rsqrt(held)
    return bf((1.0 + DECAY * root) * jnp.exp2((-DECAY * LOG2E) * root))


def norm_rows(points, first):
    wide = points.astype(jnp.float32)
    norm = jnp.sum(wide * wide, axis=0, keepdims=True)
    high = bf(norm).astype(jnp.float32)
    rest = norm - high
    mid = bf(rest).astype(jnp.float32)
    low = rest - mid
    row = iota((16, points.shape[1]), 0)
    parts = jnp.where(row == first, high, jnp.where(row == first + 1, mid, low))
    ours = (row >= first) & (row < first + 3)
    return bf(jnp.where(ours, parts, jnp.where(row < 6, 1.0, 0.0)))


def target_rows(points, eye):
    stacked = jnp.concatenate([bf(-2.0 * points.astype(jnp.float32)), norm_rows(points, 0)], axis=0)
    return bf(nt(eye, stacked))


def near_tables(near, tables):
    sub = lax.axis_index("sub")
    tables[...] = jnp.zeros_like(tables)
    entries = near[...]
    owner, leaf = entries // LEAVES, lax.rem(entries, LEAVES)
    ours = owner == sub
    least = jnp.min(jnp.where(ours, leaf, LEAVES), axis=0, keepdims=True)
    most = jnp.max(jnp.where(ours, leaf, -1), axis=0, keepdims=True)
    width = SUBS * LEAVES
    for shift in (1, 2, 4):
        least = jnp.minimum(least, pltpu.roll(least, width - shift, 1))
        most = jnp.maximum(most, pltpu.roll(most, width - shift, 1))
    tables[0:1, :] = jnp.where(least < LEAVES, least, 0)
    tables[1:2, :] = jnp.maximum(most, 0)
    mine = pltpu.roll(entries, lax.rem(width - sub * LEAVES, width), 1)[:, :128]
    mine = jnp.where(iota((NEAR, 128), 1) < LEAVES, mine, -1)
    sender = iota((SUBS, 128), 0)
    first = jnp.full((SUBS, 128), LEAVES, jnp.int32)
    rows = []
    for column in range(NEAR):
        row = mine[column:column + 1]
        rows.append((row >> 3 == sender, row & 7, row >> 3))
        first = jnp.minimum(first, jnp.where(rows[-1][0], rows[-1][1], LEAVES))
    first = jnp.min(first, axis=1, keepdims=True)
    for column, (match, leaf, owner) in enumerate(rows):
        lowest = jnp.sum(jnp.where(match, first, 0), axis=0, keepdims=True)
        slot = jnp.where(leaf == lowest, 0, 1)
        tables[2 + column:3 + column, 0:128] = jnp.where(owner >= 0, owner * CAP + slot, 0)


def prepare(points, charges, order, skeleton, interp, send_first, near_skel, tree_points, tree_charges):
    both = jnp.concatenate([points[...], charges[...]], axis=0)
    for leaf in range(LEAVES):
        row = order[:, leaf * LEAF:(leaf + 1) * LEAF]
        mine = bf(nn(both, hot(iota((PTS, LEAF), 0) == row)))
        tree_points[:, leaf * LEAF:(leaf + 1) * LEAF] = mine[:DIMS]
        tree_charges[leaf] = mine[DIMS:]
        moved = bf(nn(mine, hot(iota((LEAF, SKEL), 0) == skeleton[leaf:leaf + 1, :])))
        send_first(leaf, moved[:DIMS], bf(nt(mine[DIMS:], interp[leaf])))
        near_skel[leaf] = moved[DIMS:]


def prepare_rest(skeleton, near_rest, tree_points, tree_charges):
    below = hot(iota((LEAF, LEAF), 1) < iota((LEAF, LEAF), 0))
    ones = jnp.ones((SKEL, SKEL), jnp.bfloat16)
    for leaf in range(LEAVES):
        mine = jnp.concatenate([tree_points[:, leaf * LEAF:(leaf + 1) * LEAF], tree_charges[leaf]], axis=0)
        taken = nn(hot(iota((LEAF, SKEL), 0) == skeleton[leaf:leaf + 1, :]), ones)
        rank = nn(below, bf(1.0 - taken))
        others = (rank == iota((LEAF, SKEL), 1).astype(jnp.float32)) & (taken == 0.0)
        near_rest[leaf] = bf(nn(mine, hot(others)))


def top_message(pay, tree_points, top_interp, top_skeleton, message):
    eye = hot(iota((TOP, TOP), 0) == iota((TOP, TOP), 1))
    zeros = functools.partial(jnp.zeros, dtype=jnp.bfloat16)
    charges = jnp.concatenate([pay[leaf, DIMS:] for leaf in range(LEAVES)], axis=1)
    count = charges.shape[1]
    spread = jnp.concatenate([charges, zeros((DIMS, count)), charges, zeros((64, count))], axis=0)
    partial = nt(top_interp[...], spread)
    candidate = bf(nn(tree_points[...], hot(iota((PTS, TOP), 0) == top_skeleton[...])))
    placed = nt(eye, jnp.concatenate([zeros((RHS, TOP)), candidate, zeros((128 - RHS - DIMS, TOP))], axis=0))
    high = bf(partial)
    low = bf(partial - high.astype(jnp.float32))
    lane = iota((TOP, 128), 1)
    row = jnp.where(lane < RHS, high.astype(jnp.float32), jnp.where(lane < 48, placed, low.astype(jnp.float32)))
    for peer in range(SUBS):
        message[peer] = bf(row[peer * 8:peer * 8 + 8])


class Chain:
    def __init__(self, buf, sems, base, axis, wide, first, last, turn=0):
        self.buf, self.sems, self.base, self.turn = buf, sems, base, turn
        self.axis, self.wide, self.first, self.last = axis, wide, first, last
        self.n = NY if axis == 1 else NX
        self.steps = self.n // 2
        self.count = 2 * self.steps

    def copy(self, way, step, incoming):
        x, y = lax.axis_index("sub") // NY, lax.rem(lax.axis_index("sub"), NY)
        me = y if self.axis == 1 else x
        sign = 1 if way == 0 else -1
        back = step if incoming else step - 1
        origin = lax.rem(me - sign * back + self.n, self.n)
        to = lax.rem(me + sign + self.n, self.n)
        first, last = self.first, self.last
        if step == self.steps:
            middle = (first + last + 1) // 2
            first, last = (first, middle) if way == 0 else (middle, last)
            if first == last:
                return None
        leaves = pl.ds(first, last - first)
        if self.axis == 1:
            ref = self.buf.at[:, origin, leaves] if self.wide else self.buf.at[x, origin, leaves]
            target = x * NY + to
        else:
            ref = self.buf.at[origin, lax.rem(y + self.turn, NY), leaves]
            target = to * NY + y
        at = self.base + way * self.steps + step - 1
        send, recv = self.sems
        return pltpu.make_async_remote_copy(
            src_ref=ref, dst_ref=ref, send_sem=send.at[at], recv_sem=recv.at[at],
            device_id=(lax.axis_index("group"), target), device_id_type=MESH)

    def each(self, step, incoming):
        return [c for c in (self.copy(way, step, incoming) for way in range(2)) if c is not None]

    def start(self, step):
        for copy in self.each(step, False):
            copy.start()

    def arrive(self, step):
        for copy in self.each(step, True):
            copy.wait_recv()

    def next(self, step):
        for way in range(2):
            self.copy(way, step, True).wait_recv()
            onward = self.copy(way, step + 1, False)
            if onward is not None:
                onward.start()

    def sent(self):
        for step in range(1, self.steps + 1):
            for copy in self.each(step, False):
                copy.wait_send()


COPIES = 2 * NX // 2 + 2 * NY + NY * NX


def main(far_lists, near_lists, top_owner, top_lists,
         points, charges, order, skeleton, near_rows, interp, top_interp, top_skeleton,
         out, inverse,
         far_buf, skel_out, skel_buf, rest_out, rest_buf, rows_buf, near_skel, near_rest, far_targets, near_targets, tree_points, tree_charges, message,
         far_sum, near_sum, down_sum, shares, mine_top, pieces, packed, whole, table_rows, tables,
         send, recv, side_send, side_recv, table_sem):
    sub, group = lax.axis_index("sub"), lax.axis_index("group")
    x, y = sub // NY, lax.rem(sub, NY)

    barrier = pltpu.get_barrier_semaphore()

    def greet_sub(j, carry):
        pl.semaphore_signal(barrier, inc=1, device_id=(group, lax.rem(sub + j, SUBS)), device_id_type=MESH)
        return carry

    def greet_group(j, carry):
        pl.semaphore_signal(barrier, inc=1, device_id=(lax.rem(group + j, GROUPS), sub), device_id_type=MESH)
        return carry

    lax.fori_loop(1, SUBS, greet_sub, 0)
    lax.fori_loop(1, GROUPS, greet_group, 0)

    def send_first(leaf, skel_points, skel_charge):
        far_buf[x, y, leaf, :DIMS] = skel_points
        far_buf[x, y, leaf, DIMS:] = skel_charge

    prepare(points, charges, order, skeleton, interp, send_first, near_skel, tree_points, tree_charges)
    pl.semaphore_wait(barrier, SUBS + GROUPS - 2)

    sems = (send, recv)
    fx = Chain(far_buf, sems, 0, 0, False, 0, SPLIT)
    fy = Chain(far_buf, sems, fx.count, 1, False, SPLIT, LEAVES)
    fyy = Chain(far_buf, sems, fx.count + fy.count, 1, True, 0, SPLIT)
    base = fx.count + fy.count + fyy.count
    across = [Chain(far_buf, sems, base + turn * NX, 0, False, SPLIT, LEAVES, turn) for turn in range(NY)]

    def across_start(*turns):
        for turn in turns:
            across[turn].start(1)

    def across_next(*turns):
        for turn in turns:
            across[turn].next(1)

    def to_sub(level, src, dst):
        def go(j, carry):
            peer = lax.rem(sub + j, SUBS)
            pltpu.make_async_remote_copy(
                src_ref=src(peer), dst_ref=dst.at[sub], send_sem=side_send.at[level], recv_sem=side_recv.at[level],
                device_id=(group, peer), device_id_type=MESH).start()
            return carry
        lax.fori_loop(1, SUBS, go, 0)

    def all_of(level, dst, count):
        ref = dst.at[pl.ds(0, count)]
        return pltpu.make_async_remote_copy(
            src_ref=ref, dst_ref=ref, send_sem=side_send.at[level], recv_sem=side_recv.at[level],
            device_id=(group, lax.rem(sub + 1, SUBS)), device_id_type=MESH)

    def near_send(same_column):
        for level, out_ref, buf in ((3, skel_out, skel_buf), (4, rest_out, rest_buf)):
            def one(peer, out_ref=out_ref, buf=buf, level=level):
                pltpu.make_async_remote_copy(
                    src_ref=out_ref.at[peer], dst_ref=buf.at[sub], send_sem=side_send.at[level],
                    recv_sem=side_recv.at[level], device_id=(group, peer), device_id_type=MESH).start()

            def column(j, carry):
                one(x * NY + lax.rem(y + j, NY))
                return carry

            def others(j, carry):
                one(lax.rem((x + 1) * NY + j, SUBS))
                return carry

            if same_column:
                lax.fori_loop(1, NY, column, 0)
            else:
                lax.fori_loop(0, SUBS - NY, others, 0)

    lane = iota((8, 128), 1)

    def top_first():
        to_sub(0, lambda peer: message.at[peer], shares)

    def top_second():
        all_of(0, shares, SUBS - 1).wait_recv()
        total = shares[0].astype(jnp.float32)
        for peer in range(1, SUBS):
            total = total + shares[peer].astype(jnp.float32)
        total = total + pltpu.roll(total, 128 - 48, 1)
        chosen = shares[top_owner[0]].astype(jnp.float32)
        chunk = bf(jnp.where(lane < RHS, total, chosen))
        mine_top[...] = chunk
        pieces[group] = chunk

        def go(j, carry):
            pltpu.make_async_remote_copy(
                src_ref=mine_top, dst_ref=pieces.at[group], send_sem=side_send.at[1], recv_sem=side_recv.at[1],
                device_id=(lax.rem(group + j, GROUPS), sub), device_id_type=MESH).start()
            return carry
        lax.fori_loop(1, GROUPS, go, 0)

    def top_third():
        all_of(1, pieces, GROUPS - 1).wait_recv()
        one = pieces[top_lists[0, group]].astype(jnp.float32)
        two = pieces[top_lists[1, group]].astype(jnp.float32)
        mine = mine_top[...].astype(jnp.float32)
        row = bf(jnp.where(lane < 48, one, jnp.where(lane < 96, pltpu.roll(two, 48, 1), pltpu.roll(mine, 80, 1))))
        packed[...] = row
        whole[sub] = row
        to_sub(2, lambda peer: packed, whole)

    def fill(across_by, up_by, first, last):
        at, up = lax.rem(x + across_by, NX), lax.rem(y + up_by, NY)
        for leaf in range(first, last):
            rows_buf[at, up, leaf] = norm_rows(far_buf[at, up, leaf, :DIMS], 3)

    def fill_early(turn, carry):
        for across_by in (0, 1, NX - 1):
            fill(across_by, turn, SPLIT, LEAVES)
        return carry

    def fill_early_wide(turn, carry):
        for across_by in range(NX):
            fill(across_by, turn + NY // 2 + 1, 0, SPLIT)
        return carry

    def fill_late(turn, carry):
        fill(NX // 2, turn, SPLIT, LEAVES)
        return carry

    fx.start(1)
    fy.start(1)
    across_start(0)
    top_message(far_buf.at[x, y], tree_points, top_interp, top_skeleton, message)
    shares[sub] = message[sub]
    fx.next(1)
    top_first()
    fy.next(1)
    across_start(1, NY - 1)
    fx.arrive(2)
    fyy.start(1)
    prepare_rest(skeleton, near_rest, tree_points, tree_charges)
    near_tables(near_rows, table_rows)
    fetch = pltpu.make_async_copy(table_rows, tables, table_sem)
    fetch.start()
    across_next(0)
    eye = hot(iota((LEAF, LEAF), 0) == iota((LEAF, LEAF), 1))
    for leaf in range(LEAVES):
        far_targets[leaf] = target_rows(far_buf[x, y, leaf, :DIMS], eye[:SKEL, :SKEL])
    fy.next(2)
    across_start(2, NY - 2)
    top_second()
    fetch.wait()

    def pick_near(peer, carry):
        for slot in range(CAP):
            leaf = tables[slot, peer * LEAVES]
            skel_out[peer, slot] = near_skel[leaf]
            rest_out[peer, slot] = near_rest[leaf]
        return carry

    lax.fori_loop(0, SUBS, pick_near, 0)
    fyy.next(1)
    across_next(1, NY - 1)
    fy.next(3)
    across_start(3, NY - 3)
    for leaf in range(LEAVES):
        near_targets[leaf] = target_rows(tree_points[:, leaf * LEAF:(leaf + 1) * LEAF], eye)
    top_third()
    fyy.next(2)
    at = iota((16, PTS), 1)
    digits = bf(jnp.where(iota((16, PTS), 0) == 0, at >> 8, at & 255).astype(jnp.float32))
    for tile in range(PTS // LEAF):
        got = nt(digits, hot(iota((LEAF, PTS), 0) + tile * LEAF == order[...]))
        row = 256.0 * got[0:1] + got[1:2]
        inverse[:, tile * LEAF:(tile + 1) * LEAF] = jnp.broadcast_to(row, (8, LEAF)).astype(jnp.int32)
    fy.arrive(4)
    across_start(4)
    across_next(2, NY - 2)
    fyy.next(3)
    near_send(True)
    across_next(3, NY - 3)
    across_next(4)
    near_send(False)
    lax.fori_loop(0, NY, fill_early, 0)
    lax.fori_loop(0, NY - 1, fill_early_wide, 0)

    all_of(2, whole, SUBS - 1).wait_recv()
    table = jnp.concatenate([whole[peer].astype(jnp.float32) for peer in range(SUBS)], axis=0)
    narrow = bf(table)
    lanes = iota((TOP, 128), 1)
    squares = table * table
    square_high = bf(squares)
    square_low = bf(squares - square_high.astype(jnp.float32))
    own_norm = jnp.sum(jnp.where(lanes >= 96, squares, 0.0), axis=1, keepdims=True)
    potential = jnp.zeros((RHS, TOP), jnp.float32)
    for which in range(2):
        start = 48 * which
        points_at = (lanes >= start + RHS) & (lanes < start + 48)
        aligned = pltpu.roll(table, (start + RHS - 96) % 128, 1)
        left = bf(jnp.where(points_at, -2.0 * aligned, 0.0))
        flags = hot((iota((8, 128), 1) >= start + RHS) & (iota((8, 128), 1) < start + 48))
        other_norm = nt(flags, square_high) + nt(flags, square_low)
        values = kernel_values(nt(left, narrow) + own_norm + other_norm[:1])
        pick = hot(iota((RHS, 128), 1) == iota((RHS, 128), 0) + start)
        potential = potential + nt(bf(nt(pick, narrow)), values)
    down_sum[...] = nn(bf(potential), top_interp[...])

    fyy.arrive(4)
    for across_by in range(NX):
        fill(across_by, NY // 2, 0, SPLIT)
    for turn in range(NY):
        across[turn].arrive(2)
    lax.fori_loop(0, NY, fill_late, 0)

    def by_leaf(work, width=2):
        def several(step, carry):
            for leaf in range(width):
                work(step * width + leaf)
            return carry
        lax.fori_loop(0, LEAVES // width, several, 0)

    def place(index):
        return index >> 6, (index >> 3) & 7, index & 7

    def far_leaf(leaf):
        sources, charges = [], []
        for entry in range(FAR):
            a, b, c = place(far_lists[leaf, entry])
            got = far_buf[a, b, c]
            sources.append(jnp.concatenate([got[:DIMS], rows_buf[a, b, c]], axis=0))
            charges.append(got[DIMS:])
        values = kernel_values(nn(far_targets[leaf], jnp.concatenate(sources, axis=1)))
        far_sum[leaf] = nt(jnp.concatenate(charges, axis=1), values)

    by_leaf(far_leaf)
    def near_pass(leaf, points_of, charges_of):
        sources, charges = [], []
        for entry in range(NEAR + 1):
            if entry == 0:
                where, at = (x, y, leaf), None
            else:
                where = place(near_lists[entry - 1, sub * LEAVES + leaf])
                at = tables[entry + 1, leaf]
            sources.append(points_of(where, at, leaf))
            charges.append(charges_of(at, leaf))
        values = kernel_values(nn(near_targets[leaf], jnp.concatenate(sources, axis=1)))
        return nt(jnp.concatenate(charges, axis=1), values)

    def slot_of(at):
        return at >> 1, at & 1

    def near_first(leaf):
        def points_of(where, at, leaf):
            return jnp.concatenate([far_buf[(*where, slice(0, DIMS))], rows_buf[where]], axis=0)

        def charges_of(at, leaf):
            return near_skel[leaf] if at is None else skel_buf[slot_of(at)]

        near_sum[leaf] = near_pass(leaf, points_of, charges_of)

    def near_second(leaf):
        def both_of(at, leaf):
            return near_rest[leaf] if at is None else rest_buf[slot_of(at)]

        def points_of(where, at, leaf):
            points = both_of(at, leaf)[:DIMS]
            return jnp.concatenate([points, norm_rows(points, 3)], axis=0)

        near_sum[leaf] = near_sum[leaf] + near_pass(leaf, points_of, lambda at, leaf: both_of(at, leaf)[DIMS:])

    all_of(3, skel_buf, SUBS - 1).wait_recv()
    by_leaf(near_first)
    all_of(4, rest_buf, SUBS - 1).wait_recv()
    by_leaf(near_second)

    for leaf in range(LEAVES):
        skel_potential = bf(far_sum[leaf] + down_sum[:, leaf * SKEL:(leaf + 1) * SKEL])
        total = nn(skel_potential, interp[leaf]) + near_sum[leaf] + SHIFT * tree_charges[leaf].astype(jnp.float32)
        out[:, leaf * LEAF:(leaf + 1) * LEAF] = total

    for chain in (fx, fy, fyy, *across):
        chain.sent()
    all_of(0, shares, SUBS - 1).wait_send()
    all_of(1, pieces, GROUPS - 1).wait_send()
    all_of(2, whole, SUBS - 1).wait_send()
    all_of(3, skel_buf, SUBS - 1).wait_send()
    all_of(4, rest_buf, SUBS - 1).wait_send()


def put_back(tree, inverse, out):
    for tile in range(PTS // 128):
        lanes = pl.ds(tile * 128, 128)
        column = inverse[:, lanes]
        within, block = column & 127, column >> 7
        for half in range(RHS // 8):
            rows = pl.ds(half * 8, 8)
            got = jnp.zeros((8, 128), jnp.float32)
            for source in range(PTS // 128):
                moved = jnp.take_along_axis(tree[rows, pl.ds(source * 128, 128)], within, axis=1,
                                            mode="promise_in_bounds")
                got = jnp.where(block == source, moved, got)
            out[rows, lanes] = got


def body(points, charges, leaf_order, near_lists, far_lists, leaf_skeleton, leaf_interp, top_interp, top_skeleton,
         top_owner, top_lists):
    order = leaf_order.reshape(1, PTS)
    near = near_lists.T
    vmem, smem = pl.BlockSpec(memory_space=pltpu.VMEM), pl.BlockSpec(memory_space=pltpu.SMEM)
    shape = jax.ShapeDtypeStruct
    tree, inverse = pl.pallas_call(
        main,
        out_shape=(shape((RHS, PTS), jnp.float32), shape((8, PTS), jnp.int32)),
        in_specs=[smem] * 4 + [vmem] * 8,
        out_specs=(vmem, vmem),
        scratch_shapes=[
            pltpu.VMEM((NX, NY, LEAVES, DIMS + RHS, SKEL), jnp.bfloat16),
            pltpu.VMEM((SUBS, CAP, RHS, SKEL), jnp.bfloat16),
            pltpu.VMEM((SUBS, CAP, RHS, SKEL), jnp.bfloat16),
            pltpu.VMEM((SUBS, CAP, DIMS + RHS, SKEL), jnp.bfloat16),
            pltpu.VMEM((SUBS, CAP, DIMS + RHS, SKEL), jnp.bfloat16),
            pltpu.VMEM((NX, NY, LEAVES, 16, SKEL), jnp.bfloat16),
            pltpu.VMEM((LEAVES, RHS, SKEL), jnp.bfloat16),
            pltpu.VMEM((LEAVES, DIMS + RHS, SKEL), jnp.bfloat16),
            pltpu.VMEM((LEAVES, SKEL, DIMS + 16), jnp.bfloat16),
            pltpu.VMEM((LEAVES, LEAF, DIMS + 16), jnp.bfloat16),
            pltpu.VMEM((DIMS, PTS), jnp.bfloat16),
            pltpu.VMEM((LEAVES, RHS, LEAF), jnp.bfloat16),
            pltpu.VMEM((SUBS, 8, 128), jnp.bfloat16),
            pltpu.VMEM((LEAVES, RHS, SKEL), jnp.float32),
            pltpu.VMEM((LEAVES, RHS, LEAF), jnp.float32),
            pltpu.VMEM((RHS, LEAVES * SKEL), jnp.float32),
            pltpu.VMEM((SUBS, 8, 128), jnp.bfloat16),
            pltpu.VMEM((8, 128), jnp.bfloat16),
            pltpu.VMEM((GROUPS, 8, 128), jnp.bfloat16),
            pltpu.VMEM((8, 128), jnp.bfloat16),
            pltpu.VMEM((SUBS, 8, 128), jnp.bfloat16),
            pltpu.VMEM((16, SUBS * LEAVES), jnp.int32),
            pltpu.SMEM((16, SUBS * LEAVES), jnp.int32),
            pltpu.SemaphoreType.DMA((COPIES,)),
            pltpu.SemaphoreType.DMA((COPIES,)),
            pltpu.SemaphoreType.DMA((5,)),
            pltpu.SemaphoreType.DMA((5,)),
            pltpu.SemaphoreType.DMA,
        ],
        compiler_params=pltpu.CompilerParams(
            vmem_limit_bytes=VMEM_LIMIT, collective_id=0, has_side_effects=True),
        name="gather_and_sum",
    )(far_lists, near, top_owner, top_lists.T, points, charges, order, leaf_skeleton, near, leaf_interp, top_interp,
      top_skeleton)
    return pl.pallas_call(
        put_back,
        out_shape=shape((RHS, PTS), jnp.float32),
        in_specs=[vmem] * 2,
        out_specs=vmem,
        compiler_params=pltpu.CompilerParams(vmem_limit_bytes=VMEM_LIMIT),
        name="put_back",
    )(tree, inverse)


def solution(mesh):
    placed = (
        P(None, ("group", "sub")),
        P(None, ("group", "sub")),
        P(("group", "sub")),
        P("group", None),
        P(("group", "sub"), None),
        P(("group", "sub"), None),
        P(("group", "sub"), None, None),
        P("group", "sub"),
        P("group", None),
        P("group"),
        P(),
    )
    return jax.shard_map(
        body, mesh=mesh, in_specs=placed, out_specs=P(None, ("group", "sub")), check_vma=False
    )
```

```python
import functools

import jax
import jax.numpy as jnp
from jax import lax
from jax.experimental import pallas as pl
from jax.experimental.pallas import tpu as pltpu
from jax.sharding import PartitionSpec as P

MESH = pl.DeviceIdType.MESH
DECAY = 3.0**0.5 / 3.0
LOG2E = 1.4426950408889634
TINY = 1e-30
SHIFT = 0.5
DIMS, RHS, LEAF, SKEL, LEAVES, PTS = 32, 16, 256, 128, 8, 2048
NEAR, FAR, TOP, CAP = 7, 80, 256, 2
NX, NY, GROUPS = 4, 8, 16
SUBS = NX * NY
SPLIT = 2
VMEM_LIMIT = 56 << 20


def nn(a, b):
    return lax.dot_general(a, b, (((1,), (0,)), ((), ())), preferred_element_type=jnp.float32)


def nt(a, b):
    return lax.dot_general(a, b, (((1,), (1,)), ((), ())), preferred_element_type=jnp.float32)


def bf(a):
    return a.astype(jnp.bfloat16)


def iota(shape, axis):
    return lax.broadcasted_iota(jnp.int32, shape, axis)


def hot(mask):
    return bf(jnp.where(mask, 1.0, 0.0))


def kernel_values(distance_sq):
    held = jnp.maximum(distance_sq, TINY)
    root = held * lax.rsqrt(held)
    return bf((1.0 + DECAY * root) * jnp.exp2((-DECAY * LOG2E) * root))


def norm_rows(points, first):
    wide = points.astype(jnp.float32)
    norm = jnp.sum(wide * wide, axis=0, keepdims=True)
    high = bf(norm).astype(jnp.float32)
    rest = norm - high
    mid = bf(rest).astype(jnp.float32)
    low = rest - mid
    row = iota((16, points.shape[1]), 0)
    parts = jnp.where(row == first, high, jnp.where(row == first + 1, mid, low))
    ours = (row >= first) & (row < first + 3)
    return bf(jnp.where(ours, parts, jnp.where(row < 6, 1.0, 0.0)))


def target_rows(points, eye):
    stacked = jnp.concatenate([bf(-2.0 * points.astype(jnp.float32)), norm_rows(points, 0)], axis=0)
    return bf(nt(eye, stacked))


def near_tables(near, tables):
    sub = lax.axis_index("sub")
    tables[...] = jnp.zeros_like(tables)
    entries = near[...]
    owner, leaf = entries // LEAVES, lax.rem(entries, LEAVES)
    ours = owner == sub
    least = jnp.min(jnp.where(ours, leaf, LEAVES), axis=0, keepdims=True)
    most = jnp.max(jnp.where(ours, leaf, -1), axis=0, keepdims=True)
    width = SUBS * LEAVES
    for shift in (1, 2, 4):
        least = jnp.minimum(least, pltpu.roll(least, width - shift, 1))
        most = jnp.maximum(most, pltpu.roll(most, width - shift, 1))
    tables[0:1, :] = jnp.where(least < LEAVES, least, 0)
    tables[1:2, :] = jnp.maximum(most, 0)
    mine = pltpu.roll(entries, lax.rem(width - sub * LEAVES, width), 1)[:, :128]
    mine = jnp.where(iota((NEAR, 128), 1) < LEAVES, mine, -1)
    sender = iota((SUBS, 128), 0)
    first = jnp.full((SUBS, 128), LEAVES, jnp.int32)
    rows = []
    for column in range(NEAR):
        row = mine[column:column + 1]
        rows.append((row >> 3 == sender, row & 7, row >> 3))
        first = jnp.minimum(first, jnp.where(rows[-1][0], rows[-1][1], LEAVES))
    first = jnp.min(first, axis=1, keepdims=True)
    for column, (match, leaf, owner) in enumerate(rows):
        lowest = jnp.sum(jnp.where(match, first, 0), axis=0, keepdims=True)
        slot = jnp.where(leaf == lowest, 0, 1)
        tables[2 + column:3 + column, 0:128] = jnp.where(owner >= 0, owner * CAP + slot, 0)


def prepare(points, charges, order, skeleton, interp, send_first, near_skel, tree_points, tree_charges):
    both = jnp.concatenate([points[...], charges[...]], axis=0)
    for leaf in range(LEAVES):
        row = order[:, leaf * LEAF:(leaf + 1) * LEAF]
        mine = bf(nn(both, hot(iota((PTS, LEAF), 0) == row)))
        tree_points[:, leaf * LEAF:(leaf + 1) * LEAF] = mine[:DIMS]
        tree_charges[leaf] = mine[DIMS:]
        moved = bf(nn(mine, hot(iota((LEAF, SKEL), 0) == skeleton[leaf:leaf + 1, :])))
        send_first(leaf, moved[:DIMS], bf(nt(mine[DIMS:], interp[leaf])))
        near_skel[leaf] = moved[DIMS:]


def prepare_rest(skeleton, near_rest, tree_points, tree_charges):
    below = hot(iota((LEAF, LEAF), 1) < iota((LEAF, LEAF), 0))
    ones = jnp.ones((SKEL, SKEL), jnp.bfloat16)
    for leaf in range(LEAVES):
        mine = jnp.concatenate([tree_points[:, leaf * LEAF:(leaf + 1) * LEAF], tree_charges[leaf]], axis=0)
        taken = nn(hot(iota((LEAF, SKEL), 0) == skeleton[leaf:leaf + 1, :]), ones)
        rank = nn(below, bf(1.0 - taken))
        others = (rank == iota((LEAF, SKEL), 1).astype(jnp.float32)) & (taken == 0.0)
        near_rest[leaf] = bf(nn(mine, hot(others)))


def top_message(pay, tree_points, top_interp, top_skeleton, message):
    eye = hot(iota((TOP, TOP), 0) == iota((TOP, TOP), 1))
    zeros = functools.partial(jnp.zeros, dtype=jnp.bfloat16)
    charges = jnp.concatenate([pay[leaf, DIMS:] for leaf in range(LEAVES)], axis=1)
    count = charges.shape[1]
    spread = jnp.concatenate([charges, zeros((DIMS, count)), charges, zeros((64, count))], axis=0)
    partial = nt(top_interp[...], spread)
    candidate = bf(nn(tree_points[...], hot(iota((PTS, TOP), 0) == top_skeleton[...])))
    placed = nt(eye, jnp.concatenate([zeros((RHS, TOP)), candidate, zeros((128 - RHS - DIMS, TOP))], axis=0))
    high = bf(partial)
    low = bf(partial - high.astype(jnp.float32))
    lane = iota((TOP, 128), 1)
    row = jnp.where(lane < RHS, high.astype(jnp.float32), jnp.where(lane < 48, placed, low.astype(jnp.float32)))
    for peer in range(SUBS):
        message[peer] = bf(row[peer * 8:peer * 8 + 8])


class Chain:
    def __init__(self, buf, sems, base, axis, wide, first, last, turn=0):
        self.buf, self.sems, self.base, self.turn = buf, sems, base, turn
        self.axis, self.wide, self.first, self.last = axis, wide, first, last
        self.n = NY if axis == 1 else NX
        self.steps = self.n // 2
        self.count = 2 * self.steps

    def copy(self, way, step, incoming):
        x, y = lax.axis_index("sub") // NY, lax.rem(lax.axis_index("sub"), NY)
        me = y if self.axis == 1 else x
        sign = 1 if way == 0 else -1
        back = step if incoming else step - 1
        origin = lax.rem(me - sign * back + self.n, self.n)
        to = lax.rem(me + sign + self.n, self.n)
        first, last = self.first, self.last
        if step == self.steps:
            middle = (first + last + 1) // 2
            first, last = (first, middle) if way == 0 else (middle, last)
            if first == last:
                return None
        leaves = pl.ds(first, last - first)
        if self.axis == 1:
            ref = self.buf.at[:, origin, leaves] if self.wide else self.buf.at[x, origin, leaves]
            target = x * NY + to
        else:
            ref = self.buf.at[origin, lax.rem(y + self.turn, NY), leaves]
            target = to * NY + y
        at = self.base + way * self.steps + step - 1
        send, recv = self.sems
        return pltpu.make_async_remote_copy(
            src_ref=ref, dst_ref=ref, send_sem=send.at[at], recv_sem=recv.at[at],
            device_id=(lax.axis_index("group"), target), device_id_type=MESH)

    def each(self, step, incoming):
        return [c for c in (self.copy(way, step, incoming) for way in range(2)) if c is not None]

    def start(self, step):
        for copy in self.each(step, False):
            copy.start()

    def arrive(self, step):
        for copy in self.each(step, True):
            copy.wait_recv()

    def next(self, step):
        for way in range(2):
            self.copy(way, step, True).wait_recv()
            onward = self.copy(way, step + 1, False)
            if onward is not None:
                onward.start()

    def sent(self):
        for step in range(1, self.steps + 1):
            for copy in self.each(step, False):
                copy.wait_send()


COPIES = 2 * NX // 2 + 2 * NY + NY * NX


def main(far_lists, near_lists, top_owner, top_lists,
         points, charges, order, skeleton, near_rows, interp, top_interp, top_skeleton,
         out, inverse,
         far_buf, skel_out, skel_buf, rest_out, rest_buf, rows_buf, near_skel, near_rest, far_targets, near_targets, tree_points, tree_charges, message,
         far_sum, near_sum, down_sum, shares, mine_top, pieces, packed, whole, table_rows, tables,
         send, recv, side_send, side_recv, table_sem):
    sub, group = lax.axis_index("sub"), lax.axis_index("group")
    x, y = sub // NY, lax.rem(sub, NY)

    barrier = pltpu.get_barrier_semaphore()

    def greet_sub(j, carry):
        pl.semaphore_signal(barrier, inc=1, device_id=(group, lax.rem(sub + j, SUBS)), device_id_type=MESH)
        return carry

    def greet_group(j, carry):
        pl.semaphore_signal(barrier, inc=1, device_id=(lax.rem(group + j, GROUPS), sub), device_id_type=MESH)
        return carry

    lax.fori_loop(1, SUBS, greet_sub, 0)
    lax.fori_loop(1, GROUPS, greet_group, 0)

    def send_first(leaf, skel_points, skel_charge):
        far_buf[x, y, leaf, :DIMS] = skel_points
        far_buf[x, y, leaf, DIMS:] = skel_charge

    prepare(points, charges, order, skeleton, interp, send_first, near_skel, tree_points, tree_charges)
    pl.semaphore_wait(barrier, SUBS + GROUPS - 2)

    sems = (send, recv)
    fx = Chain(far_buf, sems, 0, 0, False, 0, SPLIT)
    fy = Chain(far_buf, sems, fx.count, 1, False, SPLIT, LEAVES)
    fyy = Chain(far_buf, sems, fx.count + fy.count, 1, True, 0, SPLIT)
    base = fx.count + fy.count + fyy.count
    across = [Chain(far_buf, sems, base + turn * NX, 0, False, SPLIT, LEAVES, turn) for turn in range(NY)]

    def across_start(*turns):
        for turn in turns:
            across[turn].start(1)

    def across_next(*turns):
        for turn in turns:
            across[turn].next(1)

    def to_sub(level, src, dst):
        def go(j, carry):
            peer = lax.rem(sub + j, SUBS)
            pltpu.make_async_remote_copy(
                src_ref=src(peer), dst_ref=dst.at[sub], send_sem=side_send.at[level], recv_sem=side_recv.at[level],
                device_id=(group, peer), device_id_type=MESH).start()
            return carry
        lax.fori_loop(1, SUBS, go, 0)

    def all_of(level, dst, count):
        ref = dst.at[pl.ds(0, count)]
        return pltpu.make_async_remote_copy(
            src_ref=ref, dst_ref=ref, send_sem=side_send.at[level], recv_sem=side_recv.at[level],
            device_id=(group, lax.rem(sub + 1, SUBS)), device_id_type=MESH)

    def near_send(same_column):
        for level, out_ref, buf in ((3, skel_out, skel_buf), (4, rest_out, rest_buf)):
            def one(peer, out_ref=out_ref, buf=buf, level=level):
                pltpu.make_async_remote_copy(
                    src_ref=out_ref.at[peer], dst_ref=buf.at[sub], send_sem=side_send.at[level],
                    recv_sem=side_recv.at[level], device_id=(group, peer), device_id_type=MESH).start()

            def column(j, carry):
                one(x * NY + lax.rem(y + j, NY))
                return carry

            def others(j, carry):
                one(lax.rem((x + 1) * NY + j, SUBS))
                return carry

            if same_column:
                lax.fori_loop(1, NY, column, 0)
            else:
                lax.fori_loop(0, SUBS - NY, others, 0)

    lane = iota((8, 128), 1)

    def top_first():
        to_sub(0, lambda peer: message.at[peer], shares)

    def top_second():
        all_of(0, shares, SUBS - 1).wait_recv()
        total = shares[0].astype(jnp.float32)
        for peer in range(1, SUBS):
            total = total + shares[peer].astype(jnp.float32)
        total = total + pltpu.roll(total, 128 - 48, 1)
        chosen = shares[top_owner[0]].astype(jnp.float32)
        chunk = bf(jnp.where(lane < RHS, total, chosen))
        mine_top[...] = chunk
        pieces[group] = chunk

        def go(j, carry):
            pltpu.make_async_remote_copy(
                src_ref=mine_top, dst_ref=pieces.at[group], send_sem=side_send.at[1], recv_sem=side_recv.at[1],
                device_id=(lax.rem(group + j, GROUPS), sub), device_id_type=MESH).start()
            return carry
        lax.fori_loop(1, GROUPS, go, 0)

    def top_third():
        all_of(1, pieces, GROUPS - 1).wait_recv()
        one = pieces[top_lists[0, group]].astype(jnp.float32)
        two = pieces[top_lists[1, group]].astype(jnp.float32)
        mine = mine_top[...].astype(jnp.float32)
        row = bf(jnp.where(lane < 48, one, jnp.where(lane < 96, pltpu.roll(two, 48, 1), pltpu.roll(mine, 80, 1))))
        packed[...] = row
        whole[sub] = row
        to_sub(2, lambda peer: packed, whole)

    def fill(across_by, up_by, first, last):
        at, up = lax.rem(x + across_by, NX), lax.rem(y + up_by, NY)
        for leaf in range(first, last):
            rows_buf[at, up, leaf] = norm_rows(far_buf[at, up, leaf, :DIMS], 3)

    def fill_early(turn, carry):
        for across_by in (0, 1, NX - 1):
            fill(across_by, turn, SPLIT, LEAVES)
        return carry

    def fill_early_wide(turn, carry):
        for across_by in range(NX):
            fill(across_by, turn + NY // 2 + 1, 0, SPLIT)
        return carry

    def fill_late(turn, carry):
        fill(NX // 2, turn, SPLIT, LEAVES)
        return carry

    fx.start(1)
    fy.start(1)
    across_start(0)
    top_message(far_buf.at[x, y], tree_points, top_interp, top_skeleton, message)
    shares[sub] = message[sub]
    fx.next(1)
    top_first()
    fy.next(1)
    across_start(1, NY - 1)
    fx.arrive(2)
    fyy.start(1)
    prepare_rest(skeleton, near_rest, tree_points, tree_charges)
    near_tables(near_rows, table_rows)
    fetch = pltpu.make_async_copy(table_rows, tables, table_sem)
    fetch.start()
    across_next(0)
    eye = hot(iota((LEAF, LEAF), 0) == iota((LEAF, LEAF), 1))
    for leaf in range(LEAVES):
        far_targets[leaf] = target_rows(far_buf[x, y, leaf, :DIMS], eye[:SKEL, :SKEL])
    fy.next(2)
    across_start(2, NY - 2)
    top_second()
    fetch.wait()

    def pick_near(peer, carry):
        for slot in range(CAP):
            leaf = tables[slot, peer * LEAVES]
            skel_out[peer, slot] = near_skel[leaf]
            rest_out[peer, slot] = near_rest[leaf]
        return carry

    lax.fori_loop(0, SUBS, pick_near, 0)
    fyy.next(1)
    across_next(1, NY - 1)
    fy.next(3)
    across_start(3, NY - 3)
    for leaf in range(LEAVES):
        near_targets[leaf] = target_rows(tree_points[:, leaf * LEAF:(leaf + 1) * LEAF], eye)
    top_third()
    fyy.next(2)
    near_send(True)
    at = iota((16, PTS), 1)
    digits = bf(jnp.where(iota((16, PTS), 0) == 0, at >> 8, at & 255).astype(jnp.float32))
    for tile in range(PTS // LEAF):
        got = nt(digits, hot(iota((LEAF, PTS), 0) + tile * LEAF == order[...]))
        row = 256.0 * got[0:1] + got[1:2]
        inverse[:, tile * LEAF:(tile + 1) * LEAF] = jnp.broadcast_to(row, (8, LEAF)).astype(jnp.int32)
    fy.arrive(4)
    across_start(4)
    across_next(2, NY - 2)
    fyy.next(3)
    across_next(3, NY - 3)
    across_next(4)
    near_send(False)
    lax.fori_loop(0, NY, fill_early, 0)
    lax.fori_loop(0, NY - 1, fill_early_wide, 0)

    all_of(2, whole, SUBS - 1).wait_recv()
    table = jnp.concatenate([whole[peer].astype(jnp.float32) for peer in range(SUBS)], axis=0)
    narrow = bf(table)
    lanes = iota((TOP, 128), 1)
    squares = table * table
    square_high = bf(squares)
    square_low = bf(squares - square_high.astype(jnp.float32))
    own_norm = jnp.sum(jnp.where(lanes >= 96, squares, 0.0), axis=1, keepdims=True)
    potential = jnp.zeros((RHS, TOP), jnp.float32)
    for which in range(2):
        start = 48 * which
        points_at = (lanes >= start + RHS) & (lanes < start + 48)
        aligned = pltpu.roll(table, (start + RHS - 96) % 128, 1)
        left = bf(jnp.where(points_at, -2.0 * aligned, 0.0))
        flags = hot((iota((8, 128), 1) >= start + RHS) & (iota((8, 128), 1) < start + 48))
        other_norm = nt(flags, square_high) + nt(flags, square_low)
        values = kernel_values(nt(left, narrow) + own_norm + other_norm[:1])
        pick = hot(iota((RHS, 128), 1) == iota((RHS, 128), 0) + start)
        potential = potential + nt(bf(nt(pick, narrow)), values)
    down_sum[...] = nn(bf(potential), top_interp[...])

    fyy.arrive(4)
    for across_by in range(NX):
        fill(across_by, NY // 2, 0, SPLIT)
    for turn in range(NY):
        across[turn].arrive(2)
    lax.fori_loop(0, NY, fill_late, 0)

    def by_leaf(work, width=2):
        def several(step, carry):
            for leaf in range(width):
                work(step * width + leaf)
            return carry
        lax.fori_loop(0, LEAVES // width, several, 0)

    def place(index):
        return index >> 6, (index >> 3) & 7, index & 7

    def far_leaf(leaf):
        sources, charges = [], []
        for entry in range(FAR):
            a, b, c = place(far_lists[leaf, entry])
            got = far_buf[a, b, c]
            sources.append(jnp.concatenate([got[:DIMS], rows_buf[a, b, c]], axis=0))
            charges.append(got[DIMS:])
        values = kernel_values(nn(far_targets[leaf], jnp.concatenate(sources, axis=1)))
        far_sum[leaf] = nt(jnp.concatenate(charges, axis=1), values)

    by_leaf(far_leaf)
    def near_pass(leaf, points_of, charges_of):
        sources, charges = [], []
        for entry in range(NEAR + 1):
            if entry == 0:
                where, at = (x, y, leaf), None
            else:
                where = place(near_lists[entry - 1, sub * LEAVES + leaf])
                at = tables[entry + 1, leaf]
            sources.append(points_of(where, at, leaf))
            charges.append(charges_of(at, leaf))
        values = kernel_values(nn(near_targets[leaf], jnp.concatenate(sources, axis=1)))
        return nt(jnp.concatenate(charges, axis=1), values)

    def slot_of(at):
        return at >> 1, at & 1

    def near_first(leaf):
        def points_of(where, at, leaf):
            return jnp.concatenate([far_buf[(*where, slice(0, DIMS))], rows_buf[where]], axis=0)

        def charges_of(at, leaf):
            return near_skel[leaf] if at is None else skel_buf[slot_of(at)]

        near_sum[leaf] = near_pass(leaf, points_of, charges_of)

    def near_second(leaf):
        def both_of(at, leaf):
            return near_rest[leaf] if at is None else rest_buf[slot_of(at)]

        def points_of(where, at, leaf):
            points = both_of(at, leaf)[:DIMS]
            return jnp.concatenate([points, norm_rows(points, 3)], axis=0)

        near_sum[leaf] = near_sum[leaf] + near_pass(leaf, points_of, lambda at, leaf: both_of(at, leaf)[DIMS:])

    all_of(3, skel_buf, SUBS - 1).wait_recv()
    by_leaf(near_first)
    all_of(4, rest_buf, SUBS - 1).wait_recv()
    by_leaf(near_second)

    for leaf in range(LEAVES):
        skel_potential = bf(far_sum[leaf] + down_sum[:, leaf * SKEL:(leaf + 1) * SKEL])
        total = nn(skel_potential, interp[leaf]) + near_sum[leaf] + SHIFT * tree_charges[leaf].astype(jnp.float32)
        out[:, leaf * LEAF:(leaf + 1) * LEAF] = total

    for chain in (fx, fy, fyy, *across):
        chain.sent()
    all_of(0, shares, SUBS - 1).wait_send()
    all_of(1, pieces, GROUPS - 1).wait_send()
    all_of(2, whole, SUBS - 1).wait_send()
    all_of(3, skel_buf, SUBS - 1).wait_send()
    all_of(4, rest_buf, SUBS - 1).wait_send()


def put_back(tree, inverse, out):
    for tile in range(PTS // 128):
        lanes = pl.ds(tile * 128, 128)
        column = inverse[:, lanes]
        within, block = column & 127, column >> 7
        for half in range(RHS // 8):
            rows = pl.ds(half * 8, 8)
            got = jnp.zeros((8, 128), jnp.float32)
            for source in range(PTS // 128):
                moved = jnp.take_along_axis(tree[rows, pl.ds(source * 128, 128)], within, axis=1,
                                            mode="promise_in_bounds")
                got = jnp.where(block == source, moved, got)
            out[rows, lanes] = got


def body(points, charges, leaf_order, near_lists, far_lists, leaf_skeleton, leaf_interp, top_interp, top_skeleton,
         top_owner, top_lists):
    order = leaf_order.reshape(1, PTS)
    near = near_lists.T
    vmem, smem = pl.BlockSpec(memory_space=pltpu.VMEM), pl.BlockSpec(memory_space=pltpu.SMEM)
    shape = jax.ShapeDtypeStruct
    tree, inverse = pl.pallas_call(
        main,
        out_shape=(shape((RHS, PTS), jnp.float32), shape((8, PTS), jnp.int32)),
        in_specs=[smem] * 4 + [vmem] * 8,
        out_specs=(vmem, vmem),
        scratch_shapes=[
            pltpu.VMEM((NX, NY, LEAVES, DIMS + RHS, SKEL), jnp.bfloat16),
            pltpu.VMEM((SUBS, CAP, RHS, SKEL), jnp.bfloat16),
            pltpu.VMEM((SUBS, CAP, RHS, SKEL), jnp.bfloat16),
            pltpu.VMEM((SUBS, CAP, DIMS + RHS, SKEL), jnp.bfloat16),
            pltpu.VMEM((SUBS, CAP, DIMS + RHS, SKEL), jnp.bfloat16),
            pltpu.VMEM((NX, NY, LEAVES, 16, SKEL), jnp.bfloat16),
            pltpu.VMEM((LEAVES, RHS, SKEL), jnp.bfloat16),
            pltpu.VMEM((LEAVES, DIMS + RHS, SKEL), jnp.bfloat16),
            pltpu.VMEM((LEAVES, SKEL, DIMS + 16), jnp.bfloat16),
            pltpu.VMEM((LEAVES, LEAF, DIMS + 16), jnp.bfloat16),
            pltpu.VMEM((DIMS, PTS), jnp.bfloat16),
            pltpu.VMEM((LEAVES, RHS, LEAF), jnp.bfloat16),
            pltpu.VMEM((SUBS, 8, 128), jnp.bfloat16),
            pltpu.VMEM((LEAVES, RHS, SKEL), jnp.float32),
            pltpu.VMEM((LEAVES, RHS, LEAF), jnp.float32),
            pltpu.VMEM((RHS, LEAVES * SKEL), jnp.float32),
            pltpu.VMEM((SUBS, 8, 128), jnp.bfloat16),
            pltpu.VMEM((8, 128), jnp.bfloat16),
            pltpu.VMEM((GROUPS, 8, 128), jnp.bfloat16),
            pltpu.VMEM((8, 128), jnp.bfloat16),
            pltpu.VMEM((SUBS, 8, 128), jnp.bfloat16),
            pltpu.VMEM((16, SUBS * LEAVES), jnp.int32),
            pltpu.SMEM((16, SUBS * LEAVES), jnp.int32),
            pltpu.SemaphoreType.DMA((COPIES,)),
            pltpu.SemaphoreType.DMA((COPIES,)),
            pltpu.SemaphoreType.DMA((5,)),
            pltpu.SemaphoreType.DMA((5,)),
            pltpu.SemaphoreType.DMA,
        ],
        compiler_params=pltpu.CompilerParams(
            vmem_limit_bytes=VMEM_LIMIT, collective_id=0, has_side_effects=True),
        name="gather_and_sum",
    )(far_lists, near, top_owner, top_lists.T, points, charges, order, leaf_skeleton, near, leaf_interp, top_interp,
      top_skeleton)
    return pl.pallas_call(
        put_back,
        out_shape=shape((RHS, PTS), jnp.float32),
        in_specs=[vmem] * 2,
        out_specs=vmem,
        compiler_params=pltpu.CompilerParams(vmem_limit_bytes=VMEM_LIMIT),
        name="put_back",
    )(tree, inverse)


def solution(mesh):
    placed = (
        P(None, ("group", "sub")),
        P(None, ("group", "sub")),
        P(("group", "sub")),
        P("group", None),
        P(("group", "sub"), None),
        P(("group", "sub"), None),
        P(("group", "sub"), None, None),
        P("group", "sub"),
        P("group", None),
        P("group"),
        P(),
    )
    return jax.shard_map(
        body, mesh=mesh, in_specs=placed, out_specs=P(None, ("group", "sub")), check_vma=False
    )
```
